128 devices in a mesh: row: 8 (over y, core), col: 16 (over x, z).
Axes of the slice: x: 4, y: 4, z: 4, core: 2. Of those that a mesh axis runs over, the one named last changes fastest.
Arguments:
- fock_tiles: bfloat16 [1024, 15, 128, 128], P(('row', 'col')), may hold values from -6 to 6
- fock_pattern: int32 [1024, 15], replicated, may hold values from -1 to 1023, as said below
- basis_tiles: bfloat16 [1024, 15, 128, 128], P(('row', 'col')), may hold values from -0.25 to 0.25
- basis_pattern: int32 [1024, 15], replicated, may hold values from -1 to 1023, as said below
- product_pattern: int32 [1024, 15], replicated, may hold values from -1 to 1023, as said below
- result_pattern: int32 [1024, 15], replicated, may hold values from -1 to 1023, as said below
- new_index: int32 [1024], replicated, may hold values from 0 to 1023, as said below
Outputs:
- fock_orth: bfloat16 [1024, 15, 128, 128], P(('row', 'col'))
The draws below stay inside these ranges and needn't reach their ends.
Inputs may be any that keep to these rules, and one draw needn't show every extreme that they name: `fock_pattern`: the filled slots of a tile row i come first and hold distinct tile columns within the (16) columns starting at min(max(i - 8, 0), 1008); slot 0 holds column i; from 10 to 15 slots of a row are filled, and the rest hold -1. `basis_pattern`: as for fock_pattern. `product_pattern`: as for fock_pattern. `result_pattern`: as for fock_pattern. `new_index`: A permutation; each tile row's new index lies in the same block of 128 consecutive tile rows and has the same remainder modulo 8; the 8 consecutive tile rows starting at a multiple of 8 move into 8 different blocks of 8 rows.
All inputs are finite; a program needn't handle non-finite values.
Results may differ from the reference program's by a relative error of at most 0.0065.
Values may be sent and summed in bfloat16 or wider, within the bound.
A program may use at most 192 MiB of HBM per device.

```python
import jax
import jax.numpy as jnp
from jax import lax

TILE = 128
RD = 8
H = 8
K = 15
NT = 1024
GROUP_ROWS = 128


def banded_pattern(key):
    rows = jnp.arange(NT, dtype=jnp.int32)
    low = jnp.clip(rows - H, 0, NT - 2 * H)
    keys = jax.random.split(jax.random.fold_in(key, 11), NT)
    scores = jax.vmap(lambda one_key: jax.random.permutation(one_key, 2 * H))(keys).astype(jnp.int32)
    spots = jnp.arange(2 * H, dtype=jnp.int32)[None, :]
    scores = jnp.where(spots == (rows - low)[:, None], -1, scores)
    picked = jnp.argsort(scores, axis=1, stable=True)[:, :K].astype(jnp.int32)
    columns = low[:, None] + picked
    regions = NT // 16 + 1
    counts = jax.random.randint(jax.random.fold_in(key, 12), (regions,), 2 * K // 3, K + 1).astype(jnp.int32)
    counts = counts.at[0].set(K)
    counts = counts.at[1].set(2 * K // 3)
    filled = counts[rows // 16]
    slots = jnp.arange(K, dtype=jnp.int32)[None, :]
    return jnp.where(slots < filled[:, None], columns, -1).astype(jnp.int32)


def draw_fock_pattern(key, part):
    return banded_pattern(jax.random.fold_in(key, 101))


def draw_basis_pattern(key, part):
    return banded_pattern(jax.random.fold_in(key, 202))


def draw_product_pattern(key, part):
    return banded_pattern(jax.random.fold_in(key, 303))


def draw_result_pattern(key, part):
    return banded_pattern(jax.random.fold_in(key, 404))


def draw_new_index(key, part):
    groups = NT // GROUP_ROWS
    width = GROUP_ROWS // RD
    keys = jax.random.split(jax.random.fold_in(key, 505), groups)

    def one_group(group_key):
        first_key, second_key, third_key = jax.random.split(group_key, 3)
        outer = jax.random.permutation(first_key, width).astype(jnp.int32)
        inner = jax.random.permutation(second_key, width).astype(jnp.int32)
        shifts = jax.random.permutation(third_key, width).astype(jnp.int32)[:RD]
        source = jnp.arange(width, dtype=jnp.int32)[:, None]
        slot = jnp.arange(RD, dtype=jnp.int32)[None, :]
        target = outer[(inner[source] + shifts[slot]) % width]
        return target * RD + slot
    local = jax.vmap(one_group)(keys)
    bases = jnp.arange(groups, dtype=jnp.int32)[:, None, None] * GROUP_ROWS
    return (local + bases).reshape(NT).astype(jnp.int32)


def steps_of(rng, extent, shards, least, top_value):
    level, own = 1.0, jax.random.fold_in(rng, 6)
    for position, parts in shards:
        steps = jnp.exp(jax.random.uniform(jax.random.fold_in(own, position), (parts,), jnp.float32, least / len(shards), top_value / len(shards)))
        level = level * jnp.repeat(steps, extent[position] // parts).reshape([-1 if axis == position else 1 for axis in range(len(extent))])
    return level


def noise(rng, extent, deviation, most, pieces=(), kind=jnp.bfloat16):
    level = steps_of(rng, extent, pieces, -0.22, 0.18) if pieces else 1.0
    drawn = jax.random.normal(rng, extent, jnp.float32) * deviation * level
    return jnp.minimum(jnp.maximum(drawn, -most), most).astype(kind)


def setup_inputs(seed: int = 0) -> dict:
    streams_of = jax.random.split(jax.random.key(seed), 8)
    fock_tiles = noise(streams_of[0], (NT, K, TILE, TILE), 1.0, 6.0, ((0, 128),))
    fock_pattern = draw_fock_pattern(jax.random.fold_in(streams_of[7], 71), 0)
    basis_tiles = noise(streams_of[2], (NT, K, TILE, TILE), (4 * TILE) ** -0.5, 0.25, ((0, 128),))
    basis_pattern = draw_basis_pattern(jax.random.fold_in(streams_of[7], 71), 0)
    product_pattern = draw_product_pattern(jax.random.fold_in(streams_of[7], 71), 0)
    result_pattern = draw_result_pattern(jax.random.fold_in(streams_of[7], 71), 0)
    new_index = draw_new_index(jax.random.fold_in(streams_of[7], 71), 0)
    return {"fock_tiles": fock_tiles, "fock_pattern": fock_pattern, "basis_tiles": basis_tiles, "basis_pattern": basis_pattern, "product_pattern": product_pattern, "result_pattern": result_pattern, "new_index": new_index}


def reference(fock_tiles, fock_pattern, basis_tiles, basis_pattern, product_pattern, result_pattern, new_index):
    span = 2 * H

    def row_step(accum, row):
        fock_row = fock_tiles[row].astype(jnp.float32)
        fock_cols = fock_pattern[row]
        basis_index = jnp.clip(fock_cols, 0, NT - 1).astype(jnp.int32)
        gathered = basis_tiles[basis_index].astype(jnp.float32)
        gathered_cols = basis_pattern[basis_index]
        prod_cols = product_pattern[row]
        match = (gathered_cols[:, None, :] == prod_cols[None, :, None]) & (prod_cols[None, :, None] >= 0) & (fock_cols[:, None, None] >= 0)
        chosen = jnp.einsum('kps,ksab->kpab', match.astype(jnp.float32), gathered)
        product_row = jnp.einsum('kab,kpbc->pac', fock_row, chosen).astype(jnp.bfloat16)
        basis_row = basis_tiles[row].astype(jnp.float32)
        targets = basis_pattern[row]
        valid = targets >= 0
        target_rows = jnp.clip(targets, 0, NT - 1).astype(jnp.int32)
        result_cols = result_pattern[target_rows]
        second = (prod_cols[None, None, :] == result_cols[:, :, None]) & (result_cols[:, :, None] >= 0) & valid[:, None, None]
        picked = jnp.einsum('srp,pab->srab', second.astype(jnp.float32), product_row.astype(jnp.float32))
        terms = jnp.einsum('sba,srbc->srac', basis_row, picked)
        terms = terms * valid.astype(jnp.float32)[:, None, None, None]
        low = jnp.clip(row - H, 0, NT - span).astype(jnp.int32)
        offsets = jnp.clip(target_rows - low, 0, span - 1).astype(jnp.int32)
        added = jnp.zeros((span,) + terms.shape[1:], jnp.float32).at[offsets].add(terms)
        window = lax.dynamic_slice_in_dim(accum, low, span, 0)
        accum = lax.dynamic_update_slice_in_dim(accum, window + added, low, 0)
        return accum, None

    start = jnp.zeros(fock_tiles.shape, jnp.float32)
    accum, unused = lax.scan(row_step, start, jnp.arange(NT, dtype=jnp.int32))
    orth = accum.astype(jnp.bfloat16)
    return jnp.zeros_like(orth).at[new_index.astype(jnp.int32)].set(orth)
```

```python
import functools

import jax
import jax.numpy as jnp
from jax import lax
from jax.experimental import pallas as pl
from jax.experimental.pallas import tpu as pltpu
from jax.sharding import PartitionSpec as P

T = 128
R = 8
K = 15
C = 24
TRI = R * (R + 1) // 2
PACK = R * R + TRI - R
VMEM_LIMIT = 60 * 1024 * 1024
BF = jnp.bfloat16
ANY = pl.BlockSpec(memory_space=pl.ANY)
SMEM = pl.BlockSpec(memory_space=pltpu.SMEM)


def up_pieces():
    pieces, off = [], 0
    for col in range(8, 16):
        pieces.append((col, 0, 8, off))
        off += 8
    for u in range(7):
        pieces.append((16 + u, u + 1, 7 - u, off))
        off += 7 - u
    return pieces


def down_pieces():
    pieces, off = [], 0
    for u in range(8):
        pieces.append((u, 0, u + 1, off))
        off += u + 1
    for col in range(8, 15):
        pieces.append((col, 0, 8, off))
        off += 8
    return pieces


def first_pieces():
    pieces, off = [], 0
    for u in range(8):
        pieces.append((16 + u, 0, u + 1, off))
        off += u + 1
    return pieces


def last_pieces():
    pieces, off = [], 0
    for u in range(7):
        pieces.append((u, u + 1, 7 - u, off))
        off += 7 - u
    return pieces


def second_pieces():
    return [(15, 0, 8, 0)]


def run_all(copies):
    for copy in copies:
        copy.start()
    for copy in copies:
        copy.wait()


def send_copies(buf, out, pieces, sem):
    return [
        pltpu.make_async_copy(buf.at[col, pl.ds(row, rows)], out.at[pl.ds(off, rows)], sem)
        for col, row, rows, off in pieces
    ]


def pack_out(device, last, buf, up, down, ext, sem):
    run_all(
        send_copies(buf, up, up_pieces(), sem) + send_copies(buf, down, down_pieces(), sem)
    )
    for which, pieces in ((0, first_pieces()), (1, second_pieces()), (last, last_pieces())):

        @pl.when(device == which)
        def _():
            run_all(send_copies(buf, ext, pieces, sem))


def scatter_start(rel, tiles, dst, base, sem):
    def row(t, carry):
        def slot(s, inner):
            col = rel[t, s]

            @pl.when(col >= 0)
            def _():
                pltpu.make_async_copy(tiles.at[t, s], dst.at[col, base + t], sem).start()

            return inner

        return lax.fori_loop(0, K, slot, carry)

    lax.fori_loop(0, R, row, 0)


def scatter_wait(rel, tiles, dst, base, sem):
    def row(t, carry):
        def slot(s, inner):
            @pl.when(rel[t, s] >= 0)
            def _():
                pltpu.make_async_copy(tiles.at[t, s], dst.at[0, base + t], sem).wait()

            return inner

        return lax.fori_loop(0, K, slot, carry)

    lax.fori_loop(0, R, row, 0)


def zero_block(ref, lead):
    def one(q, carry):
        ref[q] = jnp.zeros(ref.shape[1:], ref.dtype)
        return carry

    lax.fori_loop(0, lead, one, 0)


def pack_kernel(last, info, zrel, z, up, down, ext, buf, sem):
    zero_block(buf, C)
    scatter_start(zrel, z, buf, 0, sem)
    scatter_wait(zrel, z, buf, 0, sem)
    pack_out(info[0], last, buf, up, down, ext, sem)


def window_copies(win, low, high, sem):
    copies = []
    for col, row, rows, off in up_pieces():
        copies.append(
            pltpu.make_async_copy(low.at[pl.ds(off, rows)], win.at[col - 8, pl.ds(row, rows)], sem)
        )
    for col, row, rows, off in down_pieces():
        copies.append(
            pltpu.make_async_copy(
                high.at[pl.ds(off, rows)], win.at[col + 8, pl.ds(16 + row, rows)], sem
            )
        )
    return copies


def zero_gaps(win):
    def corner(q, carry):
        win[16 + q, pl.ds(0, 8)] = jnp.zeros((8, T, T), BF)
        win[q, pl.ds(16, 8)] = jnp.zeros((8, T, T), BF)
        return carry

    lax.fori_loop(0, 8, corner, 0)
    for u in range(8):
        win[8 + u, pl.ds(0, u + 1)] = jnp.zeros((u + 1, T, T), BF)
        if u < 7:
            win[8 + u, pl.ds(17 + u, 7 - u)] = jnp.zeros((7 - u, T, T), BF)
    win[23, pl.ds(16, 8)] = jnp.zeros((8, T, T), BF)


def edge_window(device, last, win, ext, sem):
    def fill(which, pieces, shift, base):
        @pl.when(device == which)
        def _():
            run_all(
                [
                    pltpu.make_async_copy(
                        ext.at[pl.ds(off, rows)], win.at[col + shift, pl.ds(base + row, rows)], sem
                    )
                    for col, row, rows, off in pieces
                ]
            )

    fill(1, first_pieces(), -8, 0)
    fill(0, second_pieces(), 8, 16)
    fill(last - 1, last_pieces(), 8, 16)


def band_step(left, win, pair, rows, start, depth, put):
    lhs = jnp.concatenate(
        [left[start + q, pl.ds(2 * rows, 2)].reshape(2 * T, T) for q in range(depth)], axis=1
    )
    rhs = jnp.concatenate(
        [win[2 * pair + h, pl.ds(start, depth)].reshape(depth * T, T) for h in range(2)], axis=1
    )
    total = jnp.dot(lhs, rhs, preferred_element_type=jnp.float32)
    for h in range(2):
        for m in range(2):
            put(2 * pair + h, 2 * rows + m, total[m * T : (m + 1) * T, h * T : (h + 1) * T])


def band_product(edge, left, win, put):
    @pl.when(edge == 0)
    def _():
        def pair_step(pair, carry):
            start = jnp.minimum(jnp.maximum(2 * pair - 8, 0), 6)
            low = jnp.maximum(pair - 8, 0)
            high = jnp.minimum(pair, 3)

            def rows_step(rows, inner):
                band_step(left, win, pair, rows, start, 18, put)
                return inner

            return lax.fori_loop(low, high + 1, rows_step, carry)

        lax.fori_loop(0, C // 2, pair_step, 0)

    @pl.when(edge != 0)
    def _():
        def step(q, carry):
            band_step(left, win, q // 4, lax.rem(q, 4), 0, C, put)
            return carry

        lax.fori_loop(0, C // 2 * 4, step, 0)


def first_kernel(
    last, info, zrel, frel, keep, z, f, low, high, ext,
    prod, up, down, pext, zwin, win, left, out, sem, sem2, sem3,
):
    device = info[0]
    copies = window_copies(win, low, high, sem)
    for copy in copies:
        copy.start()
    zero_gaps(win)

    def own(q, carry):
        win[q, pl.ds(8, 8)] = jnp.zeros((8, T, T), BF)
        return carry

    lax.fori_loop(0, C, own, 0)
    zero_block(left, C)
    scatter_start(zrel, z, win, 8, sem2)
    scatter_start(frel, f, left, 0, sem3)
    zero_block(out, C)
    for copy in copies:
        copy.wait()
    edge_window(device, last, win, ext, sem)
    scatter_wait(zrel, z, win, 8, sem2)
    scatter_wait(frel, f, left, 0, sem3)
    keep_win = pltpu.make_async_copy(win.at[pl.ds(8, 8)], zwin, sem)
    keep_win.start()

    def put(col, row, value):
        out[col, row] = jnp.where(keep[col, row] > 0, value, 0.0).astype(BF)

    band_product(info[1], left, win, put)
    keep_win.wait()
    whole = pltpu.make_async_copy(out, prod, sem2)
    whole.start()
    pack_out(device, last, out, up, down, pext, sem)
    whole.wait()


def turn_kernel(zwin, turned):
    for a in range(R):
        turned[0, a] = zwin[a, 0].T


def second_kernel(
    last, info, rrel, dest, prod, turned, low, high, ext, outgoing, win, left, out, sem, sem2
):
    copies = window_copies(win, low, high, sem)
    copies.append(pltpu.make_async_copy(prod, win.at[:, pl.ds(8, 8)], sem))
    copies.append(pltpu.make_async_copy(turned, left, sem))
    for copy in copies:
        copy.start()
    zero_gaps(win)
    zero_block(out, C + 1)
    for copy in copies:
        copy.wait()
    edge_window(info[0], last, win, ext, sem)

    def put(col, row, value):
        out[col, row] = value.astype(BF)

    band_product(info[1], left, win, put)

    def deliver(go):
        def row(t, carry):
            def slot(s, inner):
                copy = pltpu.make_async_copy(
                    out.at[rrel[t, s], t], outgoing.at[dest[t], s], sem2
                )
                copy.start() if go else copy.wait()
                return inner

            return lax.fori_loop(0, K, slot, carry)

        lax.fori_loop(0, R, row, 0)

    deliver(True)
    deliver(False)


def take_kernel(source, incoming, out):
    out[...] = incoming[...]


def tiles(count):
    return jax.ShapeDtypeStruct((count, T, T), BF)


def body(
    fock_tiles, fock_pattern, basis_tiles, basis_pattern, product_pattern, result_pattern, new_index
):
    total_rows = fock_pattern.shape[0]
    width = lax.axis_size("col")
    devices = lax.axis_size("row") * width
    last = devices - 1
    device = lax.axis_index(("row", "col"))
    first_row = device * R
    params = pltpu.CompilerParams(vmem_limit_bytes=VMEM_LIMIT)

    def relative(pattern, empty):
        own = lax.dynamic_slice_in_dim(pattern, first_row, R, 0)
        return jnp.where(own >= 0, own - first_row + 8, empty)

    zrel = relative(basis_pattern, -1)
    frel = relative(fock_pattern, -1)
    prel = relative(product_pattern, -1)
    rrel = relative(result_pattern, C)
    keep = jnp.any(
        prel[None] == jnp.arange(C, dtype=jnp.int32)[:, None, None], axis=-1
    ).astype(jnp.int32)
    edge = ((device < 2) | (device > last - 2)).astype(jnp.int32)
    info = jnp.stack([device.astype(jnp.int32), edge])

    axes = ("row", "col")
    rise = [(q, q + 1) for q in range(devices - 1)]
    fall = [(q + 1, q) for q in range(devices - 1)]
    ends = [(0, 1), (1, 0), (last, last - 1)]

    up, down, ext = pl.pallas_call(
        functools.partial(pack_kernel, last),
        out_shape=(tiles(PACK), tiles(PACK), tiles(TRI)),
        in_specs=[SMEM, SMEM, ANY],
        out_specs=(ANY, ANY, ANY),
        scratch_shapes=[pltpu.VMEM((C, R, T, T), BF), pltpu.SemaphoreType.DMA],
        compiler_params=params,
        name="pack",
    )(info, zrel, basis_tiles)
    low = lax.ppermute(up, axes, rise)
    high = lax.ppermute(down, axes, fall)
    ext = lax.ppermute(ext, axes, ends)

    block = jax.ShapeDtypeStruct((C, R, T, T), BF)
    prod, up, down, pext, zwin = pl.pallas_call(
        functools.partial(first_kernel, last),
        out_shape=(
            block, tiles(PACK), tiles(PACK), tiles(TRI), jax.ShapeDtypeStruct((R, C, T, T), BF)
        ),
        in_specs=[SMEM] * 4 + [ANY] * 5,
        out_specs=(ANY,) * 5,
        scratch_shapes=[
            pltpu.VMEM((C, C, T, T), BF),
            pltpu.VMEM((C, R, T, T), BF),
            pltpu.VMEM((C, R, T, T), BF),
            pltpu.SemaphoreType.DMA,
            pltpu.SemaphoreType.DMA,
            pltpu.SemaphoreType.DMA,
        ],
        compiler_params=params,
        name="first",
    )(info, zrel, frel, keep, basis_tiles, fock_tiles, low, high, ext)
    low = lax.ppermute(up, axes, rise)
    high = lax.ppermute(down, axes, fall)
    pext = lax.ppermute(pext, axes, ends)
    turned = pl.pallas_call(
        turn_kernel,
        grid=(C,),
        out_shape=block,
        in_specs=[pl.BlockSpec((R, 1, T, T), lambda q: (0, q, 0, 0))],
        out_specs=pl.BlockSpec((1, R, T, T), lambda q: (q, 0, 0, 0)),
        cost_estimate=pl.CostEstimate(
            flops=1, bytes_accessed=4 * C * R * T * T, transcendentals=0
        ),
        name="turn",
    )(zwin)

    own_new = lax.dynamic_slice_in_dim(new_index, first_row, R, 0)
    dest = own_new // R % width
    outgoing = pl.pallas_call(
        functools.partial(second_kernel, last),
        out_shape=jax.ShapeDtypeStruct((width, K, T, T), BF),
        in_specs=[SMEM] * 3 + [ANY] * 5,
        out_specs=ANY,
        scratch_shapes=[
            pltpu.VMEM((C, C, T, T), BF),
            pltpu.VMEM((C, R, T, T), BF),
            pltpu.VMEM((C + 1, R, T, T), BF),
            pltpu.SemaphoreType.DMA,
            pltpu.SemaphoreType.DMA,
        ],
        compiler_params=params,
        name="second",
    )(info, rrel, dest, prod, turned, low, high, pext)

    incoming = lax.all_to_all(outgoing, "col", split_axis=0, concat_axis=0, tiled=True)
    wanted = first_row + jnp.arange(R, dtype=jnp.int32)
    found = new_index[None, :] == wanted[:, None]
    anchor = jnp.sum(
        jnp.where(found, jnp.arange(total_rows, dtype=jnp.int32)[None, :], 0), axis=1
    )
    source = anchor // R % width
    return pl.pallas_call(
        take_kernel,
        grid_spec=pltpu.PrefetchScalarGridSpec(
            num_scalar_prefetch=1,
            grid=(R,),
            in_specs=[pl.BlockSpec((1, K, T, T), lambda q, s: (s[q], 0, 0, 0))],
            out_specs=pl.BlockSpec((1, K, T, T), lambda q, s: (q, 0, 0, 0)),
        ),
        out_shape=jax.ShapeDtypeStruct((R, K, T, T), BF),
        name="take",
    )(source, incoming)


def solution(mesh):
    placed = (
        P(("row", "col"), None, None, None),
        P(),
        P(("row", "col"), None, None, None),
        P(),
        P(),
        P(),
        P(),
    )
    return jax.shard_map(
        body,
        mesh=mesh,
        in_specs=placed,
        out_specs=P(("row", "col"), None, None, None),
        check_vma=False,
    )
```

```python
import functools

import jax
import jax.numpy as jnp
from jax import lax
from jax.experimental import pallas as pl
from jax.experimental.pallas import tpu as pltpu
from jax.sharding import PartitionSpec as P

T = 128
R = 8
K = 15
C = 24
TRI = R * (R + 1) // 2
PACK = R * R + TRI - R
VMEM_LIMIT = 63 * 1024 * 1024
BF = jnp.bfloat16
ANY = pl.BlockSpec(memory_space=pl.ANY)
SMEM = pl.BlockSpec(memory_space=pltpu.SMEM)


def up_pieces():
    pieces, off = [], 0
    for col in range(8, 16):
        pieces.append((col, 0, 8, off))
        off += 8
    for u in range(7):
        pieces.append((16 + u, u + 1, 7 - u, off))
        off += 7 - u
    return pieces


def down_pieces():
    pieces, off = [], 0
    for u in range(8):
        pieces.append((u, 0, u + 1, off))
        off += u + 1
    for col in range(8, 15):
        pieces.append((col, 0, 8, off))
        off += 8
    return pieces


def first_pieces():
    pieces, off = [], 0
    for u in range(8):
        pieces.append((16 + u, 0, u + 1, off))
        off += u + 1
    return pieces


def last_pieces():
    pieces, off = [], 0
    for u in range(7):
        pieces.append((u, u + 1, 7 - u, off))
        off += 7 - u
    return pieces


def second_pieces():
    return [(15, 0, 8, 0)]


MESH = pl.DeviceIdType.MESH
OFFSETS = (
    (0, 1), (0, 3), (1, 0), (3, 0), (1, 1), (3, 3), (1, 3), (3, 1),
    (0, 2), (2, 0), (1, 2), (3, 2), (2, 1), (2, 3), (2, 2),
)


def zero_window(win):
    def corner(q, carry):
        win[16 + q, pl.ds(0, 8)] = jnp.zeros((8, T, T), BF)
        win[q, pl.ds(16, 8)] = jnp.zeros((8, T, T), BF)
        return carry

    lax.fori_loop(0, 8, corner, 0)
    for u in range(8):
        win[8 + u, pl.ds(0, u + 1)] = jnp.zeros((u + 1, T, T), BF)
        if u < 7:
            win[8 + u, pl.ds(17 + u, 7 - u)] = jnp.zeros((7 - u, T, T), BF)
    win[23, pl.ds(16, 8)] = jnp.zeros((8, T, T), BF)


def zero_side(win, first_col, row):
    def one(q, carry):
        win[first_col + q, pl.ds(row, 8)] = jnp.zeros((8, T, T), BF)
        return carry

    lax.fori_loop(0, 16, one, 0)


def pack(table, which, raw, dst, base):
    def one(col, carry):
        for t in range(R):
            slot = table[which, col, t]
            tile = raw[jnp.maximum(slot, 0), t]
            dst[col, base + t] = jnp.where(slot >= 0, tile, jnp.zeros_like(tile))
        return carry

    lax.fori_loop(0, C, one, 0)


def band_step(left, win, pair, rows, start, depth, put):
    lhs = jnp.concatenate(
        [left[start + q, pl.ds(2 * rows, 2)].reshape(2 * T, T) for q in range(depth)], axis=1
    )
    rhs = jnp.concatenate(
        [win[2 * pair + h, pl.ds(start, depth)].reshape(depth * T, T) for h in range(2)], axis=1
    )
    total = jnp.dot(lhs, rhs, preferred_element_type=jnp.float32)
    for h in range(2):
        for m in range(2):
            put(2 * pair + h, 2 * rows + m, total[m * T : (m + 1) * T, h * T : (h + 1) * T])


def fused_kernel(
    last, width, table, rcol, srow, z, f, outgoing,
    win, pwin, left, turned, orth, sem_z, sem_f, sem_o,
    zus, zur, zds, zdr, pus, pur, pds, pdr, ezs, ezr, eps, epr,
):
    device = lax.axis_index("row") * width + lax.axis_index("col")
    has_low = device > 0
    has_high = device < last
    wide = (device < 2) | (device > last - 2)
    is_first = device == 0
    is_last = device == last

    loads = [
        pltpu.make_async_copy(z.at[t], orth.at[pl.ds(0, K), t], sem_z.at[t]) for t in range(R)
    ]
    floads = [
        pltpu.make_async_copy(f.at[t], turned.at[pl.ds(0, K), t], sem_f.at[t]) for t in range(R)
    ]
    for copy in loads + floads:
        copy.start()

    def place(dev):
        return (dev // width, lax.rem(dev, width))

    barrier = pltpu.get_barrier_semaphore()

    zero_window(win)
    zero_window(pwin)

    def clear(q, carry):
        pwin[q, pl.ds(8, 8)] = jnp.zeros((8, T, T), BF)
        pwin[16 + q, pl.ds(8, 8)] = jnp.zeros((8, T, T), BF)
        return carry

    lax.fori_loop(0, 8, clear, 0)
    orth[C] = jnp.zeros((R, T, T), BF)

    @pl.when(is_first)
    def _():
        zero_side(win, 0, 0)
        zero_side(pwin, 0, 0)

    @pl.when(is_last)
    def _():
        zero_side(win, 8, 16)
        zero_side(pwin, 8, 16)

    @pl.when(has_low)
    def _():
        pl.semaphore_signal(barrier, inc=1, device_id=place(device - 1), device_id_type=MESH)

    @pl.when(has_high)
    def _():
        pl.semaphore_signal(barrier, inc=1, device_id=place(device + 1), device_id_type=MESH)

    def send(buf, col, row, rows, to_col, to_row, ssem, rsem, dev):
        return pltpu.make_async_remote_copy(
            src_ref=buf.at[col, pl.ds(8 + row, rows)],
            dst_ref=buf.at[to_col, pl.ds(to_row, rows)],
            send_sem=ssem,
            recv_sem=rsem,
            device_id=place(dev),
            device_id_type=MESH,
        )

    def up(buf, which, ss, rs):
        col, row, rows, off = up_pieces()[which]
        return send(buf, col, row, rows, col - 8, row, ss.at[which], rs.at[which], device + 1)

    def down(buf, which, ss, rs):
        col, row, rows, off = down_pieces()[which]
        return send(buf, col, row, rows, col + 8, 16 + row, ss.at[which], rs.at[which], device - 1)

    def up_col(buf, col, ss, rs):
        return send(buf, col, 0, 8, col - 8, 0, ss.at[col - 8], rs.at[col - 8], device + 1)

    def down_col(buf, col, ss, rs):
        return send(buf, col, 0, 8, col + 8, 16, ss.at[col], rs.at[col], device - 1)

    def edge_first(buf, ss, rs):
        return [
            send(buf, col, row, rows, col - 8, row, ss.at[q], rs.at[q], device + 1)
            for q, (col, row, rows, off) in enumerate(first_pieces())
        ]

    def edge_last(buf, ss, rs):
        return [
            send(buf, col, row, rows, col + 8, 16 + row, ss.at[q], rs.at[q], device - 1)
            for q, (col, row, rows, off) in enumerate(last_pieces())
        ]

    def edge_second(buf, ss, rs):
        return [send(buf, 15, 0, 8, 23, 16, ss.at[0], rs.at[0], device - 1)]

    def start_all(copies):
        for copy in copies:
            copy.start()

    for copy in loads:
        copy.wait()
    pack(table, 0, orth, win, 8)

    @pl.when(has_low & has_high)
    def _():
        pl.semaphore_wait(barrier, 2)

    @pl.when(jnp.logical_not(has_low & has_high))
    def _():
        pl.semaphore_wait(barrier, 1)

    @pl.when(has_high)
    def _():
        start_all([up(win, q, zus, zur) for q in range(8)])

    @pl.when(has_low)
    def _():
        start_all([down(win, q, zds, zdr) for q in range(14, 7, -1)])

    @pl.when(device == 1)
    def _():
        start_all(edge_second(win, ezs, ezr))

    @pl.when(has_high)
    def _():
        start_all([up(win, q, zus, zur) for q in range(8, 15)])

    @pl.when(has_low)
    def _():
        start_all([down(win, q, zds, zdr) for q in range(7, -1, -1)])

    @pl.when(is_first)
    def _():
        start_all(edge_first(win, ezs, ezr))

    @pl.when(is_last)
    def _():
        start_all(edge_last(win, ezs, ezr))

    for copy in floads:
        copy.wait()
    pack(table, 1, turned, left, 0)

    def outer(lhs, buf, us, ur, ds, dr, es, er, put):
        def one(q, carry):
            pair = jnp.where(lax.rem(q, 2) == 0, q // 2, 11 - q // 2)

            @pl.when((pair < 4) & has_low)
            def _():
                up_col(buf, 2 * pair + 8, us, ur).wait_recv()
                up_col(buf, 2 * pair + 9, us, ur).wait_recv()

            @pl.when((pair >= 8) & has_high)
            def _():
                down_col(buf, 2 * pair - 8, ds, dr).wait_recv()

            @pl.when((pair >= 8) & (pair < 11) & has_high)
            def _():
                down_col(buf, 2 * pair - 7, ds, dr).wait_recv()

            @pl.when((pair == 11) & is_first)
            def _():
                edge_second(buf, es, er)[0].wait_recv()

            low = jnp.where(pair < 4, 0, pair - 8)
            low = jnp.where(is_first, jnp.where(pair < 4, 4, 0), low)
            low = jnp.where(is_last, jnp.where(pair < 4, 0, 4), low)
            high = jnp.where(is_first | is_last, 4, jnp.minimum(pair, 3) + 1)
            start = jnp.where(pair < 4, 0, 6)

            def rows_step(rows, inner):
                band_step(lhs, buf, pair, rows, start, 18, put)
                return inner

            return lax.fori_loop(low, high, rows_step, carry)

        lax.fori_loop(0, 8, one, 0)

    def wait_middle(buf, us, ur, ds, dr, es, er):
        @pl.when(has_low)
        def _():
            for q in range(8, 15):
                up(buf, q, us, ur).wait_recv()

        @pl.when(has_high)
        def _():
            for q in range(7, -1, -1):
                down(buf, q, ds, dr).wait_recv()

        @pl.when(device == 1)
        def _():
            for copy in edge_first(buf, es, er):
                copy.wait_recv()

        @pl.when(device == last - 1)
        def _():
            for copy in edge_last(buf, es, er):
                copy.wait_recv()

    def middle(lhs, buf, put, after):
        def one(pair, carry):
            @pl.when(jnp.logical_not(wide))
            def _():
                def rows_step(rows, inner):
                    band_step(lhs, buf, pair, rows, 2 * pair - 8, 18, put)
                    return inner

                lax.fori_loop(0, 4, rows_step, 0)

            @pl.when(wide)
            def _():
                def rows_step(rows, inner):
                    band_step(lhs, buf, pair, rows, 0, C, put)
                    return inner

                lax.fori_loop(0, 4, rows_step, 0)

            after(pair)
            return carry

        lax.fori_loop(4, 8, one, 0)

    def put_product(col, row, value):
        pwin[col, 8 + row] = jnp.where(table[2, col, row] > 0, value, 0.0).astype(BF)

    outer(left, win, zus, zur, zds, zdr, ezs, ezr, put_product)
    @pl.when(has_high)
    def _():
        start_all([up(pwin, q, pus, pur) for q in range(8, 15)])

    @pl.when(has_low)
    def _():
        start_all([down(pwin, q, pds, pdr) for q in range(7, -1, -1)])

    @pl.when(is_first)
    def _():
        start_all(edge_first(pwin, eps, epr))

    @pl.when(is_last)
    def _():
        start_all(edge_last(pwin, eps, epr))

    wait_middle(win, zus, zur, zds, zdr, ezs, ezr)

    def send_pair(pair):
        @pl.when(has_high)
        def _():
            start_all([up_col(pwin, 2 * pair + h, pus, pur) for h in range(2)])

        @pl.when(has_low)
        def _():
            down_col(pwin, 2 * pair, pds, pdr).start()

        @pl.when(has_low & (pair < 7))
        def _():
            down_col(pwin, 2 * pair + 1, pds, pdr).start()

        @pl.when((pair == 7) & (device == 1))
        def _():
            start_all(edge_second(pwin, eps, epr))

    def send_before(pair):
        @pl.when(pair > 4)
        def _():
            send_pair(pair - 1)

    middle(left, win, put_product, send_before)

    def turn(k, carry):
        for a in range(R):
            turned[k, a] = win[8 + a, k].T
        return carry

    lax.fori_loop(0, 2, turn, 0)
    send_pair(jnp.int32(7))
    lax.fori_loop(2, C, turn, 0)

    def put_orth(col, row, value):
        orth[col, row] = value.astype(BF)

    wait_middle(pwin, pus, pur, pds, pdr, eps, epr)
    middle(turned, pwin, put_orth, lambda pair: None)
    outer(turned, pwin, pus, pur, pds, pdr, eps, epr, put_orth)

    def wait_sends(buf, us, ur, ds, dr, es, er):
        @pl.when(has_high)
        def _():
            for q in range(15):
                up(buf, q, us, ur).wait_send()

        @pl.when(has_low)
        def _():
            for q in range(15):
                down(buf, q, ds, dr).wait_send()

        for which, copies in ((0, edge_first), (1, edge_second), (last, edge_last)):

            @pl.when(device == which)
            def _():
                for copy in copies(buf, es, er):
                    copy.wait_send()

    wait_sends(win, zus, zur, zds, zdr, ezs, ezr)

    def deliver(e, carry):
        row = srow[e]
        for s in range(K):
            win[e, s] = orth[rcol[row, s], row]
        return carry

    lax.fori_loop(0, width, deliver, 0)
    outs = [
        pltpu.make_async_copy(win.at[e, pl.ds(0, K)], outgoing.at[e], sem_o.at[e])
        for e in range(width)
    ]
    start_all(outs)
    wait_sends(pwin, pus, pur, pds, pdr, eps, epr)
    for copy in outs:
        copy.wait()


def exchange_kernel(width, side, source, target, bounce, ssem, rsem, lsem):
    row = lax.axis_index("row")
    col = lax.axis_index("col")
    def at(o):
        return lax.rem(col // side + o[0], side) * side + lax.rem(col + o[1], side)

    barrier = pltpu.get_barrier_semaphore()
    for o in OFFSETS:
        pl.semaphore_signal(barrier, inc=1, device_id=(row, at(o)), device_id_type=MESH)
    pl.semaphore_wait(barrier, width - 1)
    copies = []
    for q, o in enumerate(OFFSETS):
        copy = pltpu.make_async_remote_copy(
            src_ref=source.at[at(o)],
            dst_ref=target.at[col],
            send_sem=ssem.at[q],
            recv_sem=rsem.at[q],
            device_id=(row, at(o)),
            device_id_type=MESH,
        )
        copy.start()
        copies.append(copy)
    mine = pltpu.make_async_copy(source.at[col], bounce, lsem.at[0])
    mine.start()
    mine.wait()
    back = pltpu.make_async_copy(bounce, target.at[col], lsem.at[1])
    back.start()
    back.wait()
    for copy in copies:
        copy.wait()


def take_kernel(source, incoming, out):
    out[...] = incoming[...]


def body(
    fock_tiles, fock_pattern, basis_tiles, basis_pattern, product_pattern, result_pattern, new_index
):
    total_rows = fock_pattern.shape[0]
    width = lax.axis_size("col")
    last = lax.axis_size("row") * width - 1
    device = lax.axis_index(("row", "col"))
    first_row = device * R

    def relative(pattern):
        own = lax.dynamic_slice_in_dim(pattern, first_row, R, 0)
        return jnp.where(own >= 0, own - first_row + 8, C)

    patterns = jnp.stack(
        [relative(basis_pattern), relative(fock_pattern), relative(product_pattern)]
    )
    cols = jnp.arange(C, dtype=jnp.int32)[None, :, None, None]
    slots = jnp.arange(1, K + 1, dtype=jnp.int32)
    table = jnp.sum(jnp.where(patterns[:, None] == cols, slots, 0), axis=-1) - 1
    table = jnp.where(jnp.arange(3)[:, None, None] < 2, table, (table >= 0).astype(jnp.int32))
    rcol = relative(result_pattern)
    own_new = lax.dynamic_slice_in_dim(new_index, first_row, R, 0)
    dest = own_new // R % width
    srow = jnp.sum(
        jnp.where(
            dest[None, :] == jnp.arange(width, dtype=jnp.int32)[:, None],
            jnp.arange(R, dtype=jnp.int32)[None, :],
            0,
        ),
        axis=1,
    )
    dma = pltpu.SemaphoreType.DMA
    outgoing = pl.pallas_call(
        functools.partial(fused_kernel, last, width),
        out_shape=jax.ShapeDtypeStruct((width, K, T, T), BF),
        in_specs=[SMEM] * 3 + [ANY] * 2,
        out_specs=ANY,
        scratch_shapes=[
            pltpu.VMEM((C, C, T, T), BF),
            pltpu.VMEM((C, C, T, T), BF),
            pltpu.VMEM((C, R, T, T), BF),
            pltpu.VMEM((C, R, T, T), BF),
            pltpu.VMEM((C + 1, R, T, T), BF),
            dma((R,)),
            dma((R,)),
            dma((width,)),
        ]
        + [dma((15,))] * 8
        + [dma((8,))] * 4,
        compiler_params=pltpu.CompilerParams(
            vmem_limit_bytes=VMEM_LIMIT, collective_id=0, has_side_effects=True
        ),
        name="fused",
    )(table, rcol, srow, basis_tiles, fock_tiles)
    incoming = pl.pallas_call(
        functools.partial(exchange_kernel, width, 4),
        out_shape=jax.ShapeDtypeStruct((width, K, T, T), BF),
        in_specs=[ANY],
        out_specs=ANY,
        scratch_shapes=[
            pltpu.VMEM((K, T, T), BF),
            dma((width - 1,)),
            dma((width - 1,)),
            dma((2,)),
        ],
        compiler_params=pltpu.CompilerParams(collective_id=1, has_side_effects=True),
        name="exchange",
    )(outgoing)
    wanted = first_row + jnp.arange(R, dtype=jnp.int32)
    found = new_index[None, :] == wanted[:, None]
    anchor = jnp.sum(
        jnp.where(found, jnp.arange(total_rows, dtype=jnp.int32)[None, :], 0), axis=1
    )
    source = anchor // R % width
    return pl.pallas_call(
        take_kernel,
        grid_spec=pltpu.PrefetchScalarGridSpec(
            num_scalar_prefetch=1,
            grid=(R,),
            in_specs=[pl.BlockSpec((1, K, T, T), lambda q, s: (s[q], 0, 0, 0))],
            out_specs=pl.BlockSpec((1, K, T, T), lambda q, s: (q, 0, 0, 0)),
        ),
        out_shape=jax.ShapeDtypeStruct((R, K, T, T), BF),
        name="take",
    )(source, incoming)


def solution(mesh):
    placed = (
        P(("row", "col"), None, None, None),
        P(),
        P(("row", "col"), None, None, None),
        P(),
        P(),
        P(),
        P(),
    )
    return jax.shard_map(
        body,
        mesh=mesh,
        in_specs=placed,
        out_specs=P(("row", "col"), None, None, None),
        check_vma=False,
    )
```

```python
import functools

import jax
import jax.numpy as jnp
from jax import lax
from jax.experimental import pallas as pl
from jax.experimental.pallas import tpu as pltpu
from jax.sharding import PartitionSpec as P

T = 128
R = 8
K = 15
C = 24
VMEM_LIMIT = 63 * 1024 * 1024
BF = jnp.bfloat16
ANY = pl.BlockSpec(memory_space=pl.ANY)
SMEM = pl.BlockSpec(memory_space=pltpu.SMEM)


MESH = pl.DeviceIdType.MESH
OFFSETS = (
    (0, 1), (0, 3), (1, 0), (3, 0), (1, 1), (3, 3), (1, 3), (3, 1),
    (0, 2), (2, 0), (1, 2), (3, 2), (2, 1), (2, 3), (2, 2),
)


def zero_window(win, first_col, row):
    def corner(q, carry):
        win[16 + q, pl.ds(0, 8)] = jnp.zeros((8, T, T), BF)
        win[q, pl.ds(16, 8)] = jnp.zeros((8, T, T), BF)
        return carry

    lax.fori_loop(0, 8, corner, 0)
    for u in range(8):
        win[8 + u, pl.ds(0, u + 1)] = jnp.zeros((u + 1, T, T), BF)
        if u < 7:
            win[8 + u, pl.ds(17 + u, 7 - u)] = jnp.zeros((7 - u, T, T), BF)
    win[23, pl.ds(16, 8)] = jnp.zeros((8, T, T), BF)
    for q in range(8):
        win[first_col + q, row] = jnp.zeros((T, T), BF)


def zero_side(win, first_col, row):
    def one(q, carry):
        win[first_col + q, pl.ds(row, 8)] = jnp.zeros((8, T, T), BF)
        return carry

    lax.fori_loop(0, 16, one, 0)


def pack(table, which, raw, dst, base):
    def one(col, carry):
        for t in range(R):
            slot = table[which, col, t]
            tile = raw[jnp.maximum(slot, 0), t]
            dst[col, base + t] = jnp.where(slot >= 0, tile, jnp.zeros_like(tile))
        return carry

    lax.fori_loop(0, C, one, 0)


def band_step(left, win, pair, rows, start, depth, put):
    lhs = jnp.concatenate(
        [left[start + q, pl.ds(2 * rows, 2)].reshape(2 * T, T) for q in range(depth)], axis=1
    )
    rhs = jnp.concatenate(
        [win[2 * pair + h, pl.ds(start, depth)].reshape(depth * T, T) for h in range(2)], axis=1
    )
    total = jnp.dot(lhs, rhs, preferred_element_type=jnp.float32)
    for h in range(2):
        for m in range(2):
            put(2 * pair + h, 2 * rows + m, total[m * T : (m + 1) * T, h * T : (h + 1) * T])


def fused_kernel(
    last, width, side, table, rel, new_index, z, f, incoming,
    win, pwin, left, turned, orth, sem_z, sem_f, sem_o,
    zus, zur, zds, zdr, pus, pur, pds, pdr, ezs, ezr, eps, epr, xs, xr,
):
    mesh_row = lax.axis_index("row")
    mesh_col = lax.axis_index("col")
    device = mesh_row * width + mesh_col
    has_low = device > 0
    has_high = device < last
    wide = (device < 2) | (device > last - 2)
    is_first = device == 0
    is_last = device == last

    loads = [
        pltpu.make_async_copy(z.at[t], orth.at[pl.ds(0, K), t], sem_z.at[t]) for t in range(R)
    ]
    floads = [
        pltpu.make_async_copy(f.at[t], turned.at[pl.ds(0, K), t], sem_f.at[t]) for t in range(R)
    ]
    for copy in loads + floads:
        copy.start()

    def place(dev):
        return (dev // width, lax.rem(dev, width))

    def peer(o):
        col = lax.rem(mesh_col // side + o[0], side) * side + lax.rem(mesh_col + o[1], side)
        return col

    barrier = pltpu.get_barrier_semaphore()
    for o in OFFSETS:
        pl.semaphore_signal(barrier, inc=1, device_id=(mesh_row, peer(o)), device_id_type=MESH)

    zero_window(win, 16, 23)

    @pl.when(is_first)
    def _():
        zero_side(win, 0, 0)

    @pl.when(is_last)
    def _():
        zero_side(win, 8, 16)

    @pl.when(has_low)
    def _():
        pl.semaphore_signal(barrier, inc=1, device_id=place(device - 1), device_id_type=MESH)

    @pl.when(has_high)
    def _():
        pl.semaphore_signal(barrier, inc=1, device_id=place(device + 1), device_id_type=MESH)

    def send(buf, col, row, rows, to_col, to_row, ssem, rsem, dev):
        return pltpu.make_async_remote_copy(
            src_ref=buf.at[col, pl.ds(8 + row, rows)],
            dst_ref=buf.at[to_col, pl.ds(to_row, rows)],
            send_sem=ssem,
            recv_sem=rsem,
            device_id=place(dev),
            device_id_type=MESH,
        )

    def up_col(buf, col, ss, rs, skip):
        return send(
            buf, col, skip, 8 - skip, col - 8, skip, ss.at[col - 8], rs.at[col - 8], device + 1
        )

    def down_col(buf, col, ss, rs, skip):
        return send(buf, col, 0, 8 - skip, col + 8, 16, ss.at[col], rs.at[col], device - 1)

    def up_tri(buf, ss, rs):
        return [
            send(buf, 16 + u, u + 1, 7 - u, 8 + u, u + 1, ss.at[8 + u], rs.at[8 + u], device + 1)
            for u in range(7)
        ]

    def down_tri(buf, ss, rs):
        return [
            send(buf, u, 0, u + 1, 8 + u, 16, ss.at[u], rs.at[u], device - 1)
            for u in range(7, -1, -1)
        ]

    def apart(buf, first_col, cols, row, to_col, to_row, ssem, rsem, dev):
        return pltpu.make_async_remote_copy(
            src_ref=buf.at[pl.ds(first_col, cols), row],
            dst_ref=buf.at[pl.ds(to_col, cols), to_row],
            send_sem=ssem,
            recv_sem=rsem,
            device_id=place(dev),
            device_id_type=MESH,
        )

    def edge_first(buf, ss, rs):
        return [
            send(buf, 16 + u, 0, u + 1, 8 + u, 0, ss.at[u], rs.at[u], device + 1)
            for u in range(8)
        ]

    def edge_first_row(buf, ss, rs):
        return [apart(buf, 8, 8, 8, 0, 0, ss.at[8], rs.at[8], device + 1)]

    def edge_last(buf, ss, rs):
        return [
            send(buf, u, u + 1, 7 - u, 8 + u, 17 + u, ss.at[u], rs.at[u], device - 1)
            for u in range(7)
        ]

    def edge_second(buf, ss, rs):
        return [send(buf, 15, 0, 8, 23, 16, ss.at[0], rs.at[0], device - 1)]

    def edge_second_row(buf, ss, rs):
        return [apart(buf, 8, 7, 15, 16, 23, ss.at[8], rs.at[8], device - 1)]

    def start_all(copies):
        for copy in copies:
            copy.start()

    for copy in loads:
        copy.wait()
    pack(table, 0, orth, win, 8)

    @pl.when(has_low & has_high)
    def _():
        pl.semaphore_wait(barrier, width + 1)

    @pl.when(jnp.logical_not(has_low & has_high))
    def _():
        pl.semaphore_wait(barrier, width)

    @pl.when(has_high)
    def _():
        start_all([up_col(win, col, zus, zur, 0) for col in range(8, 16)])

    @pl.when(has_low)
    def _():
        start_all([down_col(win, col, zds, zdr, 1) for col in range(14, 7, -1)])

    @pl.when(device == 1)
    def _():
        start_all(edge_second(win, ezs, ezr) + edge_second_row(win, ezs, ezr))

    zero_window(pwin, 0, 0)

    def clear(q, carry):
        pwin[q, pl.ds(8, 8)] = jnp.zeros((8, T, T), BF)
        pwin[16 + q, pl.ds(8, 8)] = jnp.zeros((8, T, T), BF)
        return carry

    lax.fori_loop(0, 8, clear, 0)
    orth[C] = jnp.zeros((R, T, T), BF)

    @pl.when(is_first)
    def _():
        zero_side(pwin, 0, 0)

    @pl.when(is_last)
    def _():
        zero_side(pwin, 8, 16)

    @pl.when(has_high)
    def _():
        start_all(up_tri(win, zus, zur))

    @pl.when(has_low)
    def _():
        start_all(down_tri(win, zds, zdr))

    @pl.when(is_first)
    def _():
        start_all(edge_first(win, ezs, ezr))

    @pl.when(is_last)
    def _():
        start_all(edge_last(win, ezs, ezr))

    for copy in floads:
        copy.wait()
    pack(table, 1, turned, left, 0)

    def outer(lhs, buf, us, ur, ds, dr, es, er, put, second):
        skip_up, skip_down = (1, 0) if second else (0, 1)

        def one(q, carry):
            half = q // 2
            if second:
                pair = jnp.where(lax.rem(q, 2) == 0, 3 - half, 8 + half)
            else:
                pair = jnp.where(lax.rem(q, 2) == 0, half, 11 - half)

            @pl.when((pair < 4) & has_low)
            def _():
                up_col(buf, 2 * pair + 8, us, ur, skip_up).wait_recv()
                up_col(buf, 2 * pair + 9, us, ur, skip_up).wait_recv()

            @pl.when((pair >= 8) & has_high)
            def _():
                down_col(buf, 2 * pair - 8, ds, dr, skip_down).wait_recv()

            @pl.when((pair >= 8) & (pair < 11) & has_high)
            def _():
                down_col(buf, 2 * pair - 7, ds, dr, skip_down).wait_recv()

            if second:

                @pl.when((q == 0) & (device == 1))
                def _():
                    edge_first_row(buf, es, er)[0].wait_recv()

                @pl.when((pair == 11) & is_first)
                def _():
                    edge_second(buf, es, er)[0].wait_recv()
            else:

                @pl.when((pair == 11) & is_first)
                def _():
                    edge_second(buf, es, er)[0].wait_recv()
                    edge_second_row(buf, es, er)[0].wait_recv()

            low = jnp.where(pair < 4, 0, pair - 8)
            low = jnp.where(is_first, jnp.where(pair < 4, 4, 0), low)
            low = jnp.where(is_last, jnp.where(pair < 4, 0, 4), low)
            high = jnp.where(is_first | is_last, 4, jnp.minimum(pair, 3) + 1)
            start = jnp.where(pair < 4, 0, 6)

            def rows_step(rows, inner):
                band_step(lhs, buf, pair, rows, start, 18, put)
                return inner

            return lax.fori_loop(low, high, rows_step, carry)

        lax.fori_loop(0, 8, one, 0)

    def wait_middle(buf, us, ur, ds, dr, es, er):
        @pl.when(has_low)
        def _():
            for copy in up_tri(buf, us, ur):
                copy.wait_recv()

        @pl.when(has_high)
        def _():
            for copy in down_tri(buf, ds, dr):
                copy.wait_recv()

        @pl.when(device == 1)
        def _():
            for copy in edge_first(buf, es, er):
                copy.wait_recv()

        @pl.when(device == last - 1)
        def _():
            for copy in edge_last(buf, es, er):
                copy.wait_recv()

    def middle(lhs, buf, put, after):
        def one(q, carry):
            pair = jnp.where(lax.rem(q, 2) == 0, 7 - q // 2, 4 + q // 2)

            @pl.when(jnp.logical_not(wide))
            def _():
                def rows_step(rows, inner):
                    band_step(lhs, buf, pair, rows, 2 * pair - 8, 18, put)
                    return inner

                lax.fori_loop(0, 4, rows_step, 0)

            @pl.when(wide)
            def _():
                def rows_step(rows, inner):
                    band_step(lhs, buf, pair, rows, 0, C, put)
                    return inner

                lax.fori_loop(0, 4, rows_step, 0)

            after(q)
            return carry

        lax.fori_loop(0, 4, one, 0)

    def put_product(col, row, value):
        pwin[col, 8 + row] = jnp.where(table[2, col, row] >= 0, value, 0.0).astype(BF)

    outer(left, win, zus, zur, zds, zdr, ezs, ezr, put_product, False)

    @pl.when(has_high)
    def _():
        start_all(up_tri(pwin, pus, pur))

    @pl.when(has_low)
    def _():
        start_all(down_tri(pwin, pds, pdr))

    wait_middle(win, zus, zur, zds, zdr, ezs, ezr)

    @pl.when(is_first)
    def _():
        start_all(edge_first(pwin, eps, epr))

    @pl.when(is_last)
    def _():
        start_all(edge_last(pwin, eps, epr))

    def send_up(pair):
        @pl.when(has_high)
        def _():
            start_all([up_col(pwin, 2 * pair + h, pus, pur, 1) for h in range(2)])

    def send_down(pair):
        @pl.when(has_low)
        def _():
            down_col(pwin, 2 * pair, pds, pdr, 0).start()

        @pl.when(has_low & (pair < 7))
        def _():
            down_col(pwin, 2 * pair + 1, pds, pdr, 0).start()

    def send_ready(q):
        @pl.when(q == 1)
        def _():
            send_up(7)

            @pl.when(device == 1)
            def _():
                start_all(edge_second(pwin, eps, epr))

        @pl.when(q == 2)
        def _():
            send_down(4)

        @pl.when(q == 3)
        def _():
            send_up(6)

    middle(left, win, put_product, send_ready)

    def turn(k, carry):
        for a in range(R):
            turned[k, a] = win[8 + a, k].T
        return carry

    lax.fori_loop(0, 2, turn, 0)
    send_up(5)
    send_down(5)
    send_up(4)
    send_down(6)
    send_down(7)

    @pl.when(is_first)
    def _():
        start_all(edge_first_row(pwin, eps, epr))

    lax.fori_loop(2, C, turn, 0)

    def put_orth(col, row, value):
        orth[col, row] = value.astype(BF)

    wait_middle(pwin, pus, pur, pds, pdr, eps, epr)
    middle(turned, pwin, put_orth, lambda q: None)
    outer(turned, pwin, pus, pur, pds, pdr, eps, epr, put_orth, True)

    def wait_sends(buf, us, ur, ds, dr, es, er, product):
        def drain(copies):
            for copy in copies:
                copy.wait_send()

        @pl.when(has_high)
        def _():
            drain([up_col(buf, col, us, ur, product) for col in range(8, 16)])
            drain(up_tri(buf, us, ur))

        @pl.when(has_low)
        def _():
            drain([down_col(buf, col, ds, dr, 1 - product) for col in range(8, 15)])
            drain(down_tri(buf, ds, dr))

        @pl.when(is_first)
        def _():
            drain(edge_first(buf, es, er))
            if product:
                drain(edge_first_row(buf, es, er))

        @pl.when(device == 1)
        def _():
            drain(edge_second(buf, es, er))
            if not product:
                drain(edge_second_row(buf, es, er))

        @pl.when(is_last)
        def _():
            drain(edge_last(buf, es, er))

    def stage(e):
        row = jnp.int32(0)
        for t in range(R):
            there = lax.rem(new_index[device * R + t] // R, width)
            row = jnp.where(there == e, t, row)
        for s in range(K):
            win[e, s] = orth[rel[3, row, s], row]

    wait_sends(win, zus, zur, zds, zdr, ezs, ezr, 0)

    packets = []
    for q, o in enumerate(OFFSETS):
        stage(peer(o))
        packets.append(
            pltpu.make_async_remote_copy(
                src_ref=win.at[peer(o), pl.ds(0, K)],
                dst_ref=incoming.at[mesh_col],
                send_sem=xs.at[q],
                recv_sem=xr.at[q],
                device_id=(mesh_row, peer(o)),
                device_id_type=MESH,
            )
        )
        if q:
            packets[q - 1].start()
    stage(mesh_col)
    packets[-1].start()
    mine = pltpu.make_async_copy(win.at[mesh_col, pl.ds(0, K)], incoming.at[mesh_col], sem_o)
    mine.start()
    wait_sends(pwin, pus, pur, pds, pdr, eps, epr, 1)
    mine.wait()
    for packet in packets:
        packet.wait()


def take_kernel(width, new_index, incoming, out, held, sem_in, sem_out):
    device = lax.axis_index("row") * width + lax.axis_index("col")
    group = device // width * width

    def row(q, carry):
        def look(j, found):
            hit = new_index[(group + j) * R + q] == device * R + q
            return jnp.where(hit, j, found)

        source = lax.fori_loop(0, width, look, 0)
        pltpu.make_async_copy(incoming.at[source], held.at[q], sem_in.at[q]).start()
        return carry

    lax.fori_loop(0, R, row, 0)
    outs = []
    for q in range(R):
        pltpu.make_async_copy(incoming.at[0], held.at[q], sem_in.at[q]).wait()
        outs.append(pltpu.make_async_copy(held.at[q], out.at[q], sem_out.at[q]))
        outs[q].start()
    for copy in outs:
        copy.wait()


def body(
    fock_tiles, fock_pattern, basis_tiles, basis_pattern, product_pattern, result_pattern, new_index
):
    width = lax.axis_size("col")
    last = lax.axis_size("row") * width - 1
    device = lax.axis_index(("row", "col"))
    first_row = device * R

    def own(pattern):
        return lax.dynamic_slice_in_dim(pattern, first_row, R, 0)

    rel = jnp.stack(
        [own(basis_pattern), own(fock_pattern), own(product_pattern), own(result_pattern)]
    )
    rel = jnp.where(rel >= 0, rel - first_row + 8, C)
    cols = jnp.arange(C, dtype=jnp.int32)[None, :, None, None]
    slots = jnp.arange(1, K + 1, dtype=jnp.int32)
    table = jnp.sum(jnp.where(rel[:3, None] == cols, slots, 0), axis=-1) - 1
    dma = pltpu.SemaphoreType.DMA
    incoming = pl.pallas_call(
        functools.partial(fused_kernel, last, width, 4),
        out_shape=jax.ShapeDtypeStruct((width, K, T, T), BF),
        in_specs=[SMEM] * 3 + [ANY] * 2,
        out_specs=ANY,
        scratch_shapes=[
            pltpu.VMEM((C, C, T, T), BF),
            pltpu.VMEM((C, C, T, T), BF),
            pltpu.VMEM((C, R, T, T), BF),
            pltpu.VMEM((C, R, T, T), BF),
            pltpu.VMEM((C + 1, R, T, T), BF),
            dma((R,)),
            dma((R,)),
            dma,
        ]
        + [dma((15,))] * 8
        + [dma((9,))] * 4
        + [dma((width - 1,))] * 2,
        compiler_params=pltpu.CompilerParams(
            vmem_limit_bytes=VMEM_LIMIT, collective_id=0, has_side_effects=True
        ),
        name="fused",
    )(table, rel, new_index, basis_tiles, fock_tiles)
    return pl.pallas_call(
        functools.partial(take_kernel, width),
        out_shape=jax.ShapeDtypeStruct((R, K, T, T), BF),
        in_specs=[SMEM, ANY],
        out_specs=ANY,
        scratch_shapes=[pltpu.VMEM((R, K, T, T), BF), dma((R,)), dma((R,))],
        name="take",
    )(new_index, incoming)


def solution(mesh):
    placed = (
        P(("row", "col"), None, None, None),
        P(),
        P(("row", "col"), None, None, None),
        P(),
        P(),
        P(),
        P(),
    )
    return jax.shard_map(
        body,
        mesh=mesh,
        in_specs=placed,
        out_specs=P(("row", "col"), None, None, None),
        check_vma=False,
    )
```

```python
import functools

import jax
import jax.numpy as jnp
from jax import lax
from jax.experimental import pallas as pl
from jax.experimental.pallas import tpu as pltpu
from jax.sharding import PartitionSpec as P

T = 128
R = 8
K = 15
C = 24
VMEM_LIMIT = 63 * 1024 * 1024
BF = jnp.bfloat16
ANY = pl.BlockSpec(memory_space=pl.ANY)
SMEM = pl.BlockSpec(memory_space=pltpu.SMEM)


MESH = pl.DeviceIdType.MESH
OFFSETS = (
    (0, 1), (0, 3), (1, 0), (3, 0), (1, 1), (3, 3), (1, 3), (3, 1),
    (0, 2), (2, 0), (1, 2), (3, 2), (2, 1), (2, 3), (2, 2),
)


PARTS = 3
ROUTES = 4
FIRST = (
    tuple((("c", 23 - k, 0, 8 - k), ("c", 16 + k, 0, k + 1)) for k in range(ROUTES)),
    tuple(
        (("c", 23 - k, 0, 8 - k), ("c", 16 + k, 0, k + 1), ("r", 8 + 2 * k, 0, 2))
        for k in range(ROUTES)
    ),
)
LAST = (
    (
        (("c", 0, 1, 7),),
        (("c", 1, 2, 6), ("c", 6, 7, 1)),
        (("c", 2, 3, 5), ("c", 5, 6, 2)),
        (("c", 3, 4, 4), ("c", 4, 5, 3)),
    ),
) * 2
SECOND = (
    ((("c", 15, 0, 4),), (("c", 15, 4, 4),), (("r", 8, 7, 4),), (("r", 12, 7, 3),)),
    tuple((("c", 15, 2 * k, 2),) for k in range(ROUTES)),
)
HOLD = 11


def zero_window(win, first_col, row):
    def corner(q, carry):
        win[16 + q, pl.ds(0, 8)] = jnp.zeros((8, T, T), BF)
        win[q, pl.ds(16, 8)] = jnp.zeros((8, T, T), BF)
        return carry

    lax.fori_loop(0, 8, corner, 0)
    for u in range(8):
        win[8 + u, pl.ds(0, u + 1)] = jnp.zeros((u + 1, T, T), BF)
        if u < 7:
            win[8 + u, pl.ds(17 + u, 7 - u)] = jnp.zeros((7 - u, T, T), BF)
    win[23, pl.ds(16, 8)] = jnp.zeros((8, T, T), BF)
    for q in range(8):
        win[first_col + q, row] = jnp.zeros((T, T), BF)


def zero_side(win, first_col, row):
    def one(q, carry):
        win[first_col + q, pl.ds(row, 8)] = jnp.zeros((8, T, T), BF)
        return carry

    lax.fori_loop(0, 16, one, 0)


def pack(table, which, raw, dst, base):
    def one(col, carry):
        for t in range(R):
            slot = table[which, col, t]
            tile = raw[jnp.maximum(slot, 0), t]
            dst[col, base + t] = jnp.where(slot >= 0, tile, jnp.zeros_like(tile))
        return carry

    lax.fori_loop(0, C, one, 0)


def band_step(left, win, pair, rows, start, depth, put):
    lhs = jnp.concatenate(
        [left[start + q, pl.ds(2 * rows, 2)].reshape(2 * T, T) for q in range(depth)], axis=1
    )
    rhs = jnp.concatenate(
        [win[2 * pair + h, pl.ds(start, depth)].reshape(depth * T, T) for h in range(2)], axis=1
    )
    total = jnp.dot(lhs, rhs, preferred_element_type=jnp.float32)
    for h in range(2):
        for m in range(2):
            put(2 * pair + h, 2 * rows + m, total[m * T : (m + 1) * T, h * T : (h + 1) * T])


def fused_kernel(
    last, width, side, table, rel, new_index, z, f, incoming,
    win, pwin, left, turned, orth, sem_z, sem_f, sem_o,
    zus, zur, zds, zdr, pus, pur, pds, pdr, hold, es, er, hs, hr, xs, xr,
):
    mesh_row = lax.axis_index("row")
    mesh_col = lax.axis_index("col")
    device = mesh_row * width + mesh_col
    has_low = device > 0
    has_high = device < last
    wide = (device < 2) | (device > last - 2)
    is_first = device == 0
    is_last = device == last

    loads = [
        pltpu.make_async_copy(z.at[t], orth.at[pl.ds(0, K), t], sem_z.at[t]) for t in range(R)
    ]
    floads = [
        pltpu.make_async_copy(f.at[t], turned.at[pl.ds(0, K), t], sem_f.at[t]) for t in range(R)
    ]
    for copy in loads + floads:
        copy.start()

    def place(dev):
        return (dev // width, lax.rem(dev, width))

    def peer(o):
        col = lax.rem(mesh_col // side + o[0], side) * side + lax.rem(mesh_col + o[1], side)
        return col

    def relays(receiver):
        row, col = divmod(receiver, width)
        rows = (last + 1) // width
        return [
            row * width + (col + side) % width,
            row * width + (col - side) % width,
            (row + 2) % rows * width + col,
            (row - 2) % rows * width + col,
        ]

    flows = [(0, 1, True, FIRST), (last, last - 1, False, LAST), (1, 0, False, SECOND)]

    def pieces(flow, stage):
        return [
            (route, 3 * route + q, piece, sum(p[3] for p in group[:q]))
            for route, group in enumerate(flow[3][stage])
            for q, piece in enumerate(group)
        ]

    def part(buf, piece, shift, base):
        kind, col, row, count = piece
        if kind == "c":
            return buf.at[col + shift, pl.ds(base + row, count)]
        return buf.at[pl.ds(col + shift, count), base + row]

    def to_relay(buf, flow, stage, route, index, piece, off):
        return pltpu.make_async_remote_copy(
            src_ref=part(buf, piece, 0, 8),
            dst_ref=hold.at[stage, pl.ds(off, piece[3])],
            send_sem=es.at[stage, index],
            recv_sem=hr.at[stage, index % 3],
            device_id=divmod(relays(flow[1])[route], width),
            device_id_type=MESH,
        )

    def to_end(buf, flow, stage, index, piece, off):
        shift, base = (-8, 0) if flow[2] else (8, 16)
        return pltpu.make_async_remote_copy(
            src_ref=hold.at[stage, pl.ds(off, piece[3])],
            dst_ref=part(buf, piece, shift, base),
            send_sem=hs.at[stage, index % 3],
            recv_sem=er.at[stage, index],
            device_id=divmod(flow[1], width),
            device_id_type=MESH,
        )

    def edge_start(buf, stage, which, kinds):
        flow = flows[which]

        @pl.when(device == flow[0])
        def _():
            for route, index, piece, off in pieces(flow, stage):
                if piece[0] in kinds:
                    to_relay(buf, flow, stage, route, index, piece, off).start()

    def edge_forward(buf, stage):
        for flow in flows:
            for k, relay in enumerate(relays(flow[1])):

                @pl.when(device == relay)
                def _():
                    mine = [p for p in pieces(flow, stage) if p[0] == k]
                    for route, index, piece, off in mine:
                        to_relay(buf, flow, stage, route, index, piece, off).wait_recv()
                        to_end(buf, flow, stage, index, piece, off).start()

    def edge_receive(buf, stage, which):
        flow = flows[which]

        @pl.when(device == flow[1])
        def _():
            for route, index, piece, off in pieces(flow, stage):
                to_end(buf, flow, stage, index, piece, off).wait_recv()

    def edge_drain(buf, stage):
        for flow in flows:

            @pl.when(device == flow[0])
            def _():
                for route, index, piece, off in pieces(flow, stage):
                    to_relay(buf, flow, stage, route, index, piece, off).wait_send()

            for k, relay in enumerate(relays(flow[1])):

                @pl.when(device == relay)
                def _():
                    for route, index, piece, off in pieces(flow, stage):
                        if route == k:
                            to_end(buf, flow, stage, index, piece, off).wait_send()

    barrier = pltpu.get_barrier_semaphore()
    extra = jnp.int32(0)
    for flow in flows:
        extra = extra + jnp.where(device == flow[0], 2, 0)
        for relay in relays(flow[1])[2:]:
            extra = extra + jnp.where(device == relay, 1, 0)

            @pl.when(device == relay)
            def _():
                pl.semaphore_signal(
                    barrier, inc=1, device_id=divmod(flow[0], width), device_id_type=MESH
                )

            @pl.when(device == flow[1])
            def _():
                pl.semaphore_signal(
                    barrier, inc=1, device_id=divmod(relay, width), device_id_type=MESH
                )

    for o in OFFSETS:
        pl.semaphore_signal(barrier, inc=1, device_id=(mesh_row, peer(o)), device_id_type=MESH)

    zero_window(win, 16, 23)

    @pl.when(is_first)
    def _():
        zero_side(win, 0, 0)

    @pl.when(is_last)
    def _():
        zero_side(win, 8, 16)

    @pl.when(has_low)
    def _():
        pl.semaphore_signal(barrier, inc=1, device_id=place(device - 1), device_id_type=MESH)

    @pl.when(has_high)
    def _():
        pl.semaphore_signal(barrier, inc=1, device_id=place(device + 1), device_id_type=MESH)

    def send(buf, col, row, rows, to_col, to_row, ssem, rsem, dev):
        return pltpu.make_async_remote_copy(
            src_ref=buf.at[col, pl.ds(8 + row, rows)],
            dst_ref=buf.at[to_col, pl.ds(to_row, rows)],
            send_sem=ssem,
            recv_sem=rsem,
            device_id=place(dev),
            device_id_type=MESH,
        )

    def up_col(buf, col, ss, rs, skip):
        return send(
            buf, col, skip, 8 - skip, col - 8, skip, ss.at[col - 8], rs.at[col - 8], device + 1
        )

    def down_col(buf, col, ss, rs, skip):
        return send(buf, col, 0, 8 - skip, col + 8, 16, ss.at[col], rs.at[col], device - 1)

    def up_tri(buf, ss, rs):
        return [
            send(buf, 16 + u, u + 1, 7 - u, 8 + u, u + 1, ss.at[8 + u], rs.at[8 + u], device + 1)
            for u in range(7)
        ]

    def down_tri(buf, ss, rs):
        return [
            send(buf, u, 0, u + 1, 8 + u, 16, ss.at[u], rs.at[u], device - 1)
            for u in range(7, -1, -1)
        ]

    def start_all(copies):
        for copy in copies:
            copy.start()

    for copy in loads:
        copy.wait()
    pack(table, 0, orth, win, 8)

    neighbours = has_low.astype(jnp.int32) + has_high.astype(jnp.int32)
    pl.semaphore_wait(barrier, width - 1 + neighbours + extra)

    @pl.when(has_high)
    def _():
        start_all([up_col(win, col, zus, zur, 0) for col in range(8, 16)])

    @pl.when(has_low)
    def _():
        start_all([down_col(win, col, zds, zdr, 1) for col in range(14, 7, -1)])

    for which in range(3):
        edge_start(win, 0, which, "cr")
    zero_window(pwin, 0, 0)

    def clear(q, carry):
        pwin[q, pl.ds(8, 8)] = jnp.zeros((8, T, T), BF)
        pwin[16 + q, pl.ds(8, 8)] = jnp.zeros((8, T, T), BF)
        return carry

    lax.fori_loop(0, 8, clear, 0)
    orth[C] = jnp.zeros((R, T, T), BF)

    @pl.when(is_first)
    def _():
        zero_side(pwin, 0, 0)

    @pl.when(is_last)
    def _():
        zero_side(pwin, 8, 16)

    @pl.when(has_high)
    def _():
        start_all(up_tri(win, zus, zur))

    @pl.when(has_low)
    def _():
        start_all(down_tri(win, zds, zdr))

    for copy in floads:
        copy.wait()
    pack(table, 1, turned, left, 0)

    def outer(lhs, buf, us, ur, ds, dr, put, second):
        skip_up, skip_down = (1, 0) if second else (0, 1)

        def one(q, carry):
            half = q // 2
            if second:
                pair = jnp.where(lax.rem(q, 2) == 0, 3 - half, 8 + half)
            else:
                pair = jnp.where(lax.rem(q, 2) == 0, half, 11 - half)

            @pl.when((pair < 4) & has_low)
            def _():
                up_col(buf, 2 * pair + 8, us, ur, skip_up).wait_recv()
                up_col(buf, 2 * pair + 9, us, ur, skip_up).wait_recv()

            @pl.when((pair >= 8) & has_high)
            def _():
                down_col(buf, 2 * pair - 8, ds, dr, skip_down).wait_recv()

            @pl.when((pair >= 8) & (pair < 11) & has_high)
            def _():
                down_col(buf, 2 * pair - 7, ds, dr, skip_down).wait_recv()

            @pl.when(pair == 11)
            def _():
                edge_receive(buf, int(second), 2)

            if not second:

                @pl.when(q == 2)
                def _():
                    edge_forward(buf, 0)

            low = jnp.where(pair < 4, 0, pair - 8)
            low = jnp.where(is_first, jnp.where(pair < 4, 4, 0), low)
            low = jnp.where(is_last, jnp.where(pair < 4, 0, 4), low)
            high = jnp.where(is_first | is_last, 4, jnp.minimum(pair, 3) + 1)
            start = jnp.where(pair < 4, 0, 6)

            def rows_step(rows, inner):
                band_step(lhs, buf, pair, rows, start, 18, put)
                return inner

            return lax.fori_loop(low, high, rows_step, carry)

        lax.fori_loop(0, 8, one, 0)

    def wait_middle(buf, us, ur, ds, dr, stage):
        @pl.when(has_low)
        def _():
            for copy in up_tri(buf, us, ur):
                copy.wait_recv()

        @pl.when(has_high)
        def _():
            for copy in down_tri(buf, ds, dr):
                copy.wait_recv()

        edge_receive(buf, stage, 0)
        edge_receive(buf, stage, 1)

    def middle(lhs, buf, put, after):
        def one(q, carry):
            pair = jnp.where(lax.rem(q, 2) == 0, 7 - q // 2, 4 + q // 2)

            @pl.when(jnp.logical_not(wide))
            def _():
                def rows_step(rows, inner):
                    band_step(lhs, buf, pair, rows, 2 * pair - 8, 18, put)
                    return inner

                lax.fori_loop(0, 4, rows_step, 0)

            @pl.when(wide)
            def _():
                def rows_step(rows, inner):
                    band_step(lhs, buf, pair, rows, 0, C, put)
                    return inner

                lax.fori_loop(0, 4, rows_step, 0)

            after(q)
            return carry

        lax.fori_loop(0, 4, one, 0)

    def put_product(col, row, value):
        pwin[col, 8 + row] = jnp.where(table[2, col, row] >= 0, value, 0.0).astype(BF)

    outer(left, win, zus, zur, zds, zdr, put_product, False)

    @pl.when(has_high)
    def _():
        start_all(up_tri(pwin, pus, pur))

    @pl.when(has_low)
    def _():
        start_all(down_tri(pwin, pds, pdr))

    wait_middle(win, zus, zur, zds, zdr, 0)

    edge_start(pwin, 1, 0, "c")
    edge_start(pwin, 1, 1, "c")

    def send_up(pair):
        @pl.when(has_high)
        def _():
            start_all([up_col(pwin, 2 * pair + h, pus, pur, 1) for h in range(2)])

    def send_down(pair):
        @pl.when(has_low)
        def _():
            down_col(pwin, 2 * pair, pds, pdr, 0).start()

        @pl.when(has_low & (pair < 7))
        def _():
            down_col(pwin, 2 * pair + 1, pds, pdr, 0).start()

    def send_ready(q):
        @pl.when(q == 1)
        def _():
            send_up(7)
            edge_start(pwin, 1, 2, "c")

        @pl.when(q == 2)
        def _():
            send_down(4)

        @pl.when(q == 3)
        def _():
            send_up(6)

    middle(left, win, put_product, send_ready)

    def turn(k, carry):
        for a in range(R):
            turned[k, a] = win[8 + a, k].T
        return carry

    lax.fori_loop(0, 2, turn, 0)
    send_up(5)
    send_down(5)
    send_up(4)
    send_down(6)
    send_down(7)

    edge_start(pwin, 1, 0, "r")
    lax.fori_loop(2, C, turn, 0)
    edge_forward(pwin, 1)

    def put_orth(col, row, value):
        orth[col, row] = value.astype(BF)

    wait_middle(pwin, pus, pur, pds, pdr, 1)
    middle(turned, pwin, put_orth, lambda q: None)
    outer(turned, pwin, pus, pur, pds, pdr, put_orth, True)

    def wait_sends(buf, us, ur, ds, dr, product):
        def drain(copies):
            for copy in copies:
                copy.wait_send()

        @pl.when(has_high)
        def _():
            drain([up_col(buf, col, us, ur, product) for col in range(8, 16)])
            drain(up_tri(buf, us, ur))

        @pl.when(has_low)
        def _():
            drain([down_col(buf, col, ds, dr, 1 - product) for col in range(8, 15)])
            drain(down_tri(buf, ds, dr))

        edge_drain(buf, product)

    def stage(e):
        row = jnp.int32(0)
        for t in range(R):
            there = lax.rem(new_index[device * R + t] // R, width)
            row = jnp.where(there == e, t, row)
        for s in range(K):
            win[e, s] = orth[rel[3, row, s], row]

    wait_sends(win, zus, zur, zds, zdr, 0)

    def packet(q, p):
        there = peer(OFFSETS[q])
        slots = pl.ds(p * K // PARTS, K // PARTS)
        return pltpu.make_async_remote_copy(
            src_ref=win.at[there, slots],
            dst_ref=incoming.at[mesh_col, slots],
            send_sem=xs.at[p, q],
            recv_sem=xr.at[p, q],
            device_id=(mesh_row, there),
            device_id_type=MESH,
        )

    count = width - 1
    for q in range(count):
        stage(peer(OFFSETS[q]))
        if q:
            packet(q - 1, 0).start()
    stage(mesh_col)
    packet(count - 1, 0).start()
    for p in range(1, PARTS):
        for q in range(count):
            packet(q, p).start()
    mine = pltpu.make_async_copy(win.at[mesh_col, pl.ds(0, K)], incoming.at[mesh_col], sem_o)
    mine.start()
    wait_sends(pwin, pus, pur, pds, pdr, 1)
    mine.wait()
    for p in range(PARTS):
        for q in range(count):
            packet(q, p).wait()


def take_kernel(width, new_index, incoming, out, held, sem_in, sem_out):
    device = lax.axis_index("row") * width + lax.axis_index("col")
    group = device // width * width

    def row(q, carry):
        def look(j, found):
            hit = new_index[(group + j) * R + q] == device * R + q
            return jnp.where(hit, j, found)

        source = lax.fori_loop(0, width, look, 0)
        pltpu.make_async_copy(incoming.at[source], held.at[q], sem_in.at[q]).start()
        return carry

    lax.fori_loop(0, R, row, 0)
    outs = []
    for q in range(R):
        pltpu.make_async_copy(incoming.at[0], held.at[q], sem_in.at[q]).wait()
        outs.append(pltpu.make_async_copy(held.at[q], out.at[q], sem_out.at[q]))
        outs[q].start()
    for copy in outs:
        copy.wait()


def body(
    fock_tiles, fock_pattern, basis_tiles, basis_pattern, product_pattern, result_pattern, new_index
):
    width = lax.axis_size("col")
    last = lax.axis_size("row") * width - 1
    device = lax.axis_index(("row", "col"))
    first_row = device * R

    def own(pattern):
        return lax.dynamic_slice_in_dim(pattern, first_row, R, 0)

    rel = jnp.stack(
        [own(basis_pattern), own(fock_pattern), own(product_pattern), own(result_pattern)]
    )
    rel = jnp.where(rel >= 0, rel - first_row + 8, C)
    cols = jnp.arange(C, dtype=jnp.int32)[None, :, None, None]
    slots = jnp.arange(1, K + 1, dtype=jnp.int32)
    table = jnp.sum(jnp.where(rel[:3, None] == cols, slots, 0), axis=-1) - 1
    dma = pltpu.SemaphoreType.DMA
    incoming = pl.pallas_call(
        functools.partial(fused_kernel, last, width, 4),
        out_shape=jax.ShapeDtypeStruct((width, K, T, T), BF),
        in_specs=[SMEM] * 3 + [ANY] * 2,
        out_specs=ANY,
        scratch_shapes=[
            pltpu.VMEM((C, C, T, T), BF),
            pltpu.VMEM((C, C, T, T), BF),
            pltpu.VMEM((C, R, T, T), BF),
            pltpu.VMEM((C, R, T, T), BF),
            pltpu.VMEM((C + 1, R, T, T), BF),
            dma((R,)),
            dma((R,)),
            dma,
        ]
        + [dma((15,))] * 8
        + [pltpu.VMEM((2, HOLD, T, T), BF)]
        + [dma((2, 3 * ROUTES))] * 2
        + [dma((2, 3))] * 2
        + [dma((PARTS, width - 1))] * 2,
        compiler_params=pltpu.CompilerParams(
            vmem_limit_bytes=VMEM_LIMIT, collective_id=0, has_side_effects=True
        ),
        name="fused",
    )(table, rel, new_index, basis_tiles, fock_tiles)
    return pl.pallas_call(
        functools.partial(take_kernel, width),
        out_shape=jax.ShapeDtypeStruct((R, K, T, T), BF),
        in_specs=[SMEM, ANY],
        out_specs=ANY,
        scratch_shapes=[pltpu.VMEM((R, K, T, T), BF), dma((R,)), dma((R,))],
        name="take",
    )(new_index, incoming)


def solution(mesh):
    placed = (
        P(("row", "col"), None, None, None),
        P(),
        P(("row", "col"), None, None, None),
        P(),
        P(),
        P(),
        P(),
    )
    return jax.shard_map(
        body,
        mesh=mesh,
        in_specs=placed,
        out_specs=P(("row", "col"), None, None, None),
        check_vma=False,
    )
```

```python
import functools

import jax
import jax.numpy as jnp
from jax import lax
from jax.experimental import pallas as pl
from jax.experimental.pallas import tpu as pltpu
from jax.sharding import PartitionSpec as P

T = 128
R = 8
K = 15
C = 24
VMEM_LIMIT = 63 * 1024 * 1024
BF = jnp.bfloat16
ANY = pl.BlockSpec(memory_space=pl.ANY)
SMEM = pl.BlockSpec(memory_space=pltpu.SMEM)


MESH = pl.DeviceIdType.MESH
OFFSETS = (
    (0, 1), (0, 3), (1, 0), (3, 0), (1, 1), (3, 3), (1, 3), (3, 1),
    (0, 2), (2, 0), (1, 2), (3, 2), (2, 1), (2, 3), (2, 2),
)


PARTS = 5
ROUTES = 4
FIRST = (
    tuple((("c", 23 - k, 0, 8 - k), ("c", 16 + k, 0, k + 1)) for k in range(ROUTES)),
    tuple(
        (("c", 23 - k, 0, 8 - k), ("c", 16 + k, 0, k + 1), ("r", 8 + 2 * k, 0, 2))
        for k in range(ROUTES)
    ),
)
LAST = (
    (
        (("c", 0, 1, 7),),
        (("c", 1, 2, 6), ("c", 6, 7, 1)),
        (("c", 2, 3, 5), ("c", 5, 6, 2)),
        (("c", 3, 4, 4), ("c", 4, 5, 3)),
    ),
) * 2
SECOND = (
    ((("c", 15, 0, 4),), (("c", 15, 4, 4),), (("r", 8, 7, 4),), (("r", 12, 7, 3),)),
    tuple((("c", 15, 2 * k, 2),) for k in range(ROUTES)),
)
HOLD = 11


def zero_window(win, first_col, row):
    def corner(q, carry):
        win[16 + q, pl.ds(0, 8)] = jnp.zeros((8, T, T), BF)
        win[q, pl.ds(16, 8)] = jnp.zeros((8, T, T), BF)
        return carry

    lax.fori_loop(0, 8, corner, 0)
    for u in range(8):
        win[8 + u, pl.ds(0, u + 1)] = jnp.zeros((u + 1, T, T), BF)
        if u < 7:
            win[8 + u, pl.ds(17 + u, 7 - u)] = jnp.zeros((7 - u, T, T), BF)
    win[23, pl.ds(16, 8)] = jnp.zeros((8, T, T), BF)
    for q in range(8):
        win[first_col + q, row] = jnp.zeros((T, T), BF)


def zero_side(win, first_col, row):
    def one(q, carry):
        win[first_col + q, pl.ds(row, 8)] = jnp.zeros((8, T, T), BF)
        return carry

    lax.fori_loop(0, 16, one, 0)


def pack(table, which, raw, dst, base, first, end):
    def one(col, carry):
        for t in range(R):
            slot = table[which, col, t]
            tile = raw[jnp.maximum(slot, 0), t]
            dst[col, base + t] = jnp.where(slot >= 0, tile, jnp.zeros_like(tile))
        return carry

    lax.fori_loop(first, end, one, 0)


def band_step(left, win, pair, rows, start, depth, put):
    lhs = jnp.concatenate(
        [left[start + q, pl.ds(2 * rows, 2)].reshape(2 * T, T) for q in range(depth)], axis=1
    )
    rhs = jnp.concatenate(
        [win[2 * pair + h, pl.ds(start, depth)].reshape(depth * T, T) for h in range(2)], axis=1
    )
    total = jnp.dot(lhs, rhs, preferred_element_type=jnp.float32)
    for h in range(2):
        for m in range(2):
            put(2 * pair + h, 2 * rows + m, total[m * T : (m + 1) * T, h * T : (h + 1) * T])


def fused_kernel(
    last, width, side, table, rel, new_index, z, f, incoming,
    win, pwin, left, turned, orth, sem_z, sem_f, sem_o,
    zus, zur, zds, zdr, pus, pur, pds, pdr, hold, es, er, hs, hr, xs, xr, ready,
):
    mesh_row = lax.axis_index("row")
    mesh_col = lax.axis_index("col")
    device = mesh_row * width + mesh_col
    has_low = device > 0
    has_high = device < last
    wide = (device < 2) | (device > last - 2)
    is_first = device == 0
    is_last = device == last

    loads = [
        pltpu.make_async_copy(z.at[t], orth.at[pl.ds(0, K), t], sem_z.at[t]) for t in range(R)
    ]
    floads = [
        pltpu.make_async_copy(f.at[t], turned.at[pl.ds(0, K), t], sem_f.at[t]) for t in range(R)
    ]
    for copy in loads:
        copy.start()

    def place(dev):
        return (dev // width, lax.rem(dev, width))

    def peer(o):
        col = lax.rem(mesh_col // side + o[0], side) * side + lax.rem(mesh_col + o[1], side)
        return col

    def relays(receiver):
        row, col = divmod(receiver, width)
        rows = (last + 1) // width
        return [
            row * width + (col + side) % width,
            row * width + (col - side) % width,
            (row + 2) % rows * width + col,
            (row - 2) % rows * width + col,
        ]

    flows = [(0, 1, True, FIRST), (last, last - 1, False, LAST), (1, 0, False, SECOND)]

    def pieces(flow, stage):
        return [
            (route, 3 * route + q, piece, sum(p[3] for p in group[:q]))
            for route, group in enumerate(flow[3][stage])
            for q, piece in enumerate(group)
        ]

    def part(buf, piece, shift, base):
        kind, col, row, count = piece
        if kind == "c":
            return buf.at[col + shift, pl.ds(base + row, count)]
        return buf.at[pl.ds(col + shift, count), base + row]

    def to_relay(buf, flow, stage, route, index, piece, off):
        return pltpu.make_async_remote_copy(
            src_ref=part(buf, piece, 0, 8),
            dst_ref=hold.at[stage, pl.ds(off, piece[3])],
            send_sem=es.at[stage, index],
            recv_sem=hr.at[stage, index % 3],
            device_id=divmod(relays(flow[1])[route], width),
            device_id_type=MESH,
        )

    def to_end(buf, flow, stage, index, piece, off):
        shift, base = (-8, 0) if flow[2] else (8, 16)
        return pltpu.make_async_remote_copy(
            src_ref=hold.at[stage, pl.ds(off, piece[3])],
            dst_ref=part(buf, piece, shift, base),
            send_sem=hs.at[stage, index % 3],
            recv_sem=er.at[stage, index],
            device_id=divmod(flow[1], width),
            device_id_type=MESH,
        )

    def edge_start(buf, stage, which, kinds):
        flow = flows[which]

        @pl.when(device == flow[0])
        def _():
            for route, index, piece, off in pieces(flow, stage):
                if piece[0] in kinds:
                    to_relay(buf, flow, stage, route, index, piece, off).start()

    def edge_forward(buf, stage):
        for flow in flows:
            for k, relay in enumerate(relays(flow[1])):

                @pl.when(device == relay)
                def _():
                    mine = [p for p in pieces(flow, stage) if p[0] == k]
                    for route, index, piece, off in mine:
                        to_relay(buf, flow, stage, route, index, piece, off).wait_recv()
                        to_end(buf, flow, stage, index, piece, off).start()

    def edge_receive(buf, stage, which):
        flow = flows[which]

        @pl.when(device == flow[1])
        def _():
            for route, index, piece, off in pieces(flow, stage):
                to_end(buf, flow, stage, index, piece, off).wait_recv()

    def edge_drain(buf, stage):
        for flow in flows:

            @pl.when(device == flow[0])
            def _():
                for route, index, piece, off in pieces(flow, stage):
                    to_relay(buf, flow, stage, route, index, piece, off).wait_send()

            for k, relay in enumerate(relays(flow[1])):

                @pl.when(device == relay)
                def _():
                    for route, index, piece, off in pieces(flow, stage):
                        if route == k:
                            to_end(buf, flow, stage, index, piece, off).wait_send()

    barrier = pltpu.get_barrier_semaphore()
    extra = jnp.int32(0)
    for flow in flows:
        extra = extra + jnp.where(device == flow[0], 2, 0)
        for relay in relays(flow[1])[2:]:
            extra = extra + jnp.where(device == relay, 1, 0)

            @pl.when(device == relay)
            def _():
                pl.semaphore_signal(
                    barrier, inc=1, device_id=divmod(flow[0], width), device_id_type=MESH
                )

            @pl.when(device == flow[1])
            def _():
                pl.semaphore_signal(
                    barrier, inc=1, device_id=divmod(relay, width), device_id_type=MESH
                )

    for o in OFFSETS:
        pl.semaphore_signal(barrier, inc=1, device_id=(mesh_row, peer(o)), device_id_type=MESH)

    zero_window(win, 16, 23)

    @pl.when(is_first)
    def _():
        zero_side(win, 0, 0)

    @pl.when(is_last)
    def _():
        zero_side(win, 8, 16)

    @pl.when(has_low)
    def _():
        pl.semaphore_signal(barrier, inc=1, device_id=place(device - 1), device_id_type=MESH)

    @pl.when(has_high)
    def _():
        pl.semaphore_signal(barrier, inc=1, device_id=place(device + 1), device_id_type=MESH)

    def send(buf, col, row, rows, to_col, to_row, ssem, rsem, dev):
        return pltpu.make_async_remote_copy(
            src_ref=buf.at[col, pl.ds(8 + row, rows)],
            dst_ref=buf.at[to_col, pl.ds(to_row, rows)],
            send_sem=ssem,
            recv_sem=rsem,
            device_id=place(dev),
            device_id_type=MESH,
        )

    def up_col(buf, col, ss, rs, skip):
        return send(
            buf, col, skip, 8 - skip, col - 8, skip, ss.at[col - 8], rs.at[col - 8], device + 1
        )

    def down_col(buf, col, ss, rs, skip):
        return send(buf, col, 0, 8 - skip, col + 8, 16, ss.at[col], rs.at[col], device - 1)

    def up_tri(buf, ss, rs):
        return [
            send(buf, 16 + u, u + 1, 7 - u, 8 + u, u + 1, ss.at[8 + u], rs.at[8 + u], device + 1)
            for u in range(7)
        ]

    def down_tri(buf, ss, rs):
        return [
            send(buf, u, 0, u + 1, 8 + u, 16, ss.at[u], rs.at[u], device - 1)
            for u in range(7, -1, -1)
        ]

    def start_all(copies):
        for copy in copies:
            copy.start()

    for copy in loads:
        copy.wait()
    for copy in floads:
        copy.start()
    pack(table, 0, orth, win, 8, 8, 16)

    neighbours = has_low.astype(jnp.int32) + has_high.astype(jnp.int32)
    pl.semaphore_wait(barrier, width - 1 + neighbours + extra)

    @pl.when(has_high)
    def _():
        start_all([up_col(win, col, zus, zur, 0) for col in range(8, 16)])

    @pl.when(has_low)
    def _():
        start_all([down_col(win, col, zds, zdr, 1) for col in range(14, 7, -1)])

    pack(table, 0, orth, win, 8, 0, 8)
    pack(table, 0, orth, win, 8, 16, C)
    for which in range(3):
        edge_start(win, 0, which, "cr")

    zero_window(pwin, 0, 0)

    def clear(q, carry):
        pwin[q, pl.ds(8, 8)] = jnp.zeros((8, T, T), BF)
        pwin[16 + q, pl.ds(8, 8)] = jnp.zeros((8, T, T), BF)
        return carry

    lax.fori_loop(0, 8, clear, 0)
    orth[C] = jnp.zeros((R, T, T), BF)

    @pl.when(is_first)
    def _():
        zero_side(pwin, 0, 0)

    @pl.when(is_last)
    def _():
        zero_side(pwin, 8, 16)

    @pl.when(has_high)
    def _():
        start_all(up_tri(win, zus, zur))

    @pl.when(has_low)
    def _():
        start_all(down_tri(win, zds, zdr))

    for copy in floads:
        copy.wait()
    pack(table, 1, turned, left, 0, 0, C)

    def outer(lhs, buf, us, ur, ds, dr, put, second):
        skip_up, skip_down = (1, 0) if second else (0, 1)

        def one(q, carry):
            half = q // 2
            if second:
                pair = jnp.where(lax.rem(q, 2) == 0, 3 - half, 8 + half)
            else:
                pair = jnp.where(lax.rem(q, 2) == 0, half, 11 - half)

            @pl.when((pair < 4) & has_low)
            def _():
                up_col(buf, 2 * pair + 8, us, ur, skip_up).wait_recv()
                up_col(buf, 2 * pair + 9, us, ur, skip_up).wait_recv()

            @pl.when((pair >= 8) & has_high)
            def _():
                down_col(buf, 2 * pair - 8, ds, dr, skip_down).wait_recv()

            @pl.when((pair >= 8) & (pair < 11) & has_high)
            def _():
                down_col(buf, 2 * pair - 7, ds, dr, skip_down).wait_recv()

            @pl.when(pair == 11)
            def _():
                edge_receive(buf, int(second), 2)

            if not second:

                @pl.when(q == 2)
                def _():
                    edge_forward(buf, 0)

            low = jnp.where(pair < 4, 0, pair - 8)
            low = jnp.where(is_first, jnp.where(pair < 4, 4, 0), low)
            low = jnp.where(is_last, jnp.where(pair < 4, 0, 4), low)
            high = jnp.where(is_first | is_last, 4, jnp.minimum(pair, 3) + 1)
            start = jnp.where(pair < 4, 0, 6)

            def rows_step(rows, inner):
                band_step(lhs, buf, pair, rows, start, 18, put)
                return inner

            return lax.fori_loop(low, high, rows_step, carry)

        lax.fori_loop(0, 8, one, 0)

    def wait_middle(buf, us, ur, ds, dr, stage):
        @pl.when(has_low)
        def _():
            for copy in up_tri(buf, us, ur):
                copy.wait_recv()

        @pl.when(has_high)
        def _():
            for copy in down_tri(buf, ds, dr):
                copy.wait_recv()

        edge_receive(buf, stage, 0)
        edge_receive(buf, stage, 1)

    def middle(lhs, buf, put, after):
        def one(q, carry):
            pair = jnp.where(lax.rem(q, 2) == 0, 7 - q // 2, 4 + q // 2)

            @pl.when(jnp.logical_not(wide))
            def _():
                def rows_step(rows, inner):
                    band_step(lhs, buf, pair, rows, 2 * pair - 8, 18, put)
                    return inner

                lax.fori_loop(0, 4, rows_step, 0)

            @pl.when(wide)
            def _():
                def rows_step(rows, inner):
                    band_step(lhs, buf, pair, rows, 0, C, put)
                    return inner

                lax.fori_loop(0, 4, rows_step, 0)

            after(q)
            return carry

        lax.fori_loop(0, 4, one, 0)

    def put_product(col, row, value):
        pwin[col, 8 + row] = jnp.where(table[2, col, row] >= 0, value, 0.0).astype(BF)

    outer(left, win, zus, zur, zds, zdr, put_product, False)

    @pl.when(has_high)
    def _():
        start_all(up_tri(pwin, pus, pur))

    @pl.when(has_low)
    def _():
        start_all(down_tri(pwin, pds, pdr))

    wait_middle(win, zus, zur, zds, zdr, 0)

    edge_start(pwin, 1, 0, "c")
    edge_start(pwin, 1, 1, "c")

    def send_up(pair):
        @pl.when(has_high)
        def _():
            start_all([up_col(pwin, 2 * pair + h, pus, pur, 1) for h in range(2)])

    def send_down(pair):
        @pl.when(has_low)
        def _():
            down_col(pwin, 2 * pair, pds, pdr, 0).start()

        @pl.when(has_low & (pair < 7))
        def _():
            down_col(pwin, 2 * pair + 1, pds, pdr, 0).start()

    def send_ready(q):
        @pl.when(q == 1)
        def _():
            send_up(7)
            edge_start(pwin, 1, 2, "c")

        @pl.when(q == 2)
        def _():
            send_down(4)

        @pl.when(q == 3)
        def _():
            send_up(6)

    middle(left, win, put_product, send_ready)

    def turn(k, carry):
        for a in range(R):
            turned[k, a] = win[8 + a, k].T
        return carry

    lax.fori_loop(0, 2, turn, 0)
    send_up(5)
    send_down(5)
    send_up(4)
    send_down(6)
    send_down(7)

    edge_start(pwin, 1, 0, "r")
    lax.fori_loop(2, C, turn, 0)
    edge_forward(pwin, 1)

    def put_orth(col, row, value):
        orth[col, row] = value.astype(BF)

    wait_middle(pwin, pus, pur, pds, pdr, 1)
    middle(turned, pwin, put_orth, lambda q: None)
    outer(turned, pwin, pus, pur, pds, pdr, put_orth, True)

    def wait_sends(buf, us, ur, ds, dr, product):
        def drain(copies):
            for copy in copies:
                copy.wait_send()

        @pl.when(has_high)
        def _():
            drain([up_col(buf, col, us, ur, product) for col in range(8, 16)])
            drain(up_tri(buf, us, ur))

        @pl.when(has_low)
        def _():
            drain([down_col(buf, col, ds, dr, 1 - product) for col in range(8, 15)])
            drain(down_tri(buf, ds, dr))

        edge_drain(buf, product)

    def stage(e):
        row = jnp.int32(0)
        for t in range(R):
            there = lax.rem(new_index[device * R + t] // R, width)
            row = jnp.where(there == e, t, row)
        for s in range(K):
            win[e, s] = orth[rel[3, row, s], row]

    wait_sends(win, zus, zur, zds, zdr, 0)

    def packet(q, p):
        there = peer(OFFSETS[q])
        slots = pl.ds(p * K // PARTS, K // PARTS)
        return pltpu.make_async_remote_copy(
            src_ref=win.at[there, slots],
            dst_ref=incoming.at[mesh_col, slots],
            send_sem=xs.at[p, q],
            recv_sem=xr.at[p, q],
            device_id=(mesh_row, there),
            device_id_type=MESH,
        )

    count = width - 1
    for o in OFFSETS:
        pl.semaphore_signal(ready, inc=1, device_id=(mesh_row, peer(o)), device_id_type=MESH)
    for q in range(count):
        stage(peer(OFFSETS[q]))
    stage(mesh_col)
    pl.semaphore_wait(ready, count)
    for p in range(PARTS):
        for q in range(count):
            packet(q, p).start()
    mine = pltpu.make_async_copy(win.at[mesh_col, pl.ds(0, K)], incoming.at[mesh_col], sem_o)
    mine.start()
    wait_sends(pwin, pus, pur, pds, pdr, 1)
    mine.wait()
    for p in range(PARTS):
        for q in range(count):
            packet(q, p).wait()


def take_kernel(width, new_index, incoming, out, held, sem_in, sem_out):
    device = lax.axis_index("row") * width + lax.axis_index("col")
    group = device // width * width

    def row(q, carry):
        def look(j, found):
            hit = new_index[(group + j) * R + q] == device * R + q
            return jnp.where(hit, j, found)

        source = lax.fori_loop(0, width, look, 0)
        pltpu.make_async_copy(incoming.at[source], held.at[q], sem_in.at[q]).start()
        return carry

    lax.fori_loop(0, R, row, 0)
    outs = []
    for q in range(R):
        pltpu.make_async_copy(incoming.at[0], held.at[q], sem_in.at[q]).wait()
        outs.append(pltpu.make_async_copy(held.at[q], out.at[q], sem_out.at[q]))
        outs[q].start()
    for copy in outs:
        copy.wait()


def body(
    fock_tiles, fock_pattern, basis_tiles, basis_pattern, product_pattern, result_pattern, new_index
):
    width = lax.axis_size("col")
    last = lax.axis_size("row") * width - 1
    device = lax.axis_index(("row", "col"))
    first_row = device * R

    def own(pattern):
        return lax.dynamic_slice_in_dim(pattern, first_row, R, 0)

    rel = jnp.stack(
        [own(basis_pattern), own(fock_pattern), own(product_pattern), own(result_pattern)]
    )
    rel = jnp.where(rel >= 0, rel - first_row + 8, C)
    cols = jnp.arange(C, dtype=jnp.int32)[None, :, None, None]
    slots = jnp.arange(1, K + 1, dtype=jnp.int32)
    table = jnp.sum(jnp.where(rel[:3, None] == cols, slots, 0), axis=-1) - 1
    dma = pltpu.SemaphoreType.DMA
    incoming = pl.pallas_call(
        functools.partial(fused_kernel, last, width, 4),
        out_shape=jax.ShapeDtypeStruct((width, K, T, T), BF),
        in_specs=[SMEM] * 3 + [ANY] * 2,
        out_specs=ANY,
        scratch_shapes=[
            pltpu.VMEM((C, C, T, T), BF),
            pltpu.VMEM((C, C, T, T), BF),
            pltpu.VMEM((C, R, T, T), BF),
            pltpu.VMEM((C, R, T, T), BF),
            pltpu.VMEM((C + 1, R, T, T), BF),
            dma((R,)),
            dma((R,)),
            dma,
        ]
        + [dma((15,))] * 8
        + [pltpu.VMEM((2, HOLD, T, T), BF)]
        + [dma((2, 3 * ROUTES))] * 2
        + [dma((2, 3))] * 2
        + [dma((PARTS, width - 1))] * 2
        + [pltpu.SemaphoreType.REGULAR],
        compiler_params=pltpu.CompilerParams(
            vmem_limit_bytes=VMEM_LIMIT, collective_id=0, has_side_effects=True
        ),
        name="fused",
    )(table, rel, new_index, basis_tiles, fock_tiles)
    return pl.pallas_call(
        functools.partial(take_kernel, width),
        out_shape=jax.ShapeDtypeStruct((R, K, T, T), BF),
        in_specs=[SMEM, ANY],
        out_specs=ANY,
        scratch_shapes=[pltpu.VMEM((R, K, T, T), BF), dma((R,)), dma((R,))],
        name="take",
    )(new_index, incoming)


def solution(mesh):
    placed = (
        P(("row", "col"), None, None, None),
        P(),
        P(("row", "col"), None, None, None),
        P(),
        P(),
        P(),
        P(),
    )
    return jax.shard_map(
        body,
        mesh=mesh,
        in_specs=placed,
        out_specs=P(("row", "col"), None, None, None),
        check_vma=False,
    )
```

```python
import functools

import jax
import jax.numpy as jnp
from jax import lax
from jax.experimental import pallas as pl
from jax.experimental.pallas import tpu as pltpu
from jax.sharding import PartitionSpec as P

T = 128
R = 8
K = 15
C = 24
VMEM_LIMIT = 63 * 1024 * 1024
BF = jnp.bfloat16
ANY = pl.BlockSpec(memory_space=pl.ANY)
SMEM = pl.BlockSpec(memory_space=pltpu.SMEM)


MESH = pl.DeviceIdType.MESH
OFFSETS = (
    (0, 1), (0, 3), (1, 0), (3, 0), (1, 1), (3, 3), (1, 3), (3, 1),
    (0, 2), (2, 0), (1, 2), (3, 2), (2, 1), (2, 3), (2, 2),
)


PARTS = 5
ROUTES = 4
FIRST = (
    tuple((("c", 23 - k, 0, 8 - k), ("c", 16 + k, 0, k + 1)) for k in range(ROUTES)),
    tuple(
        (("c", 23 - k, 0, 8 - k), ("c", 16 + k, 0, k + 1), ("r", 8 + 2 * k, 0, 2))
        for k in range(ROUTES)
    ),
)
LAST = (
    (
        (("c", 0, 1, 7),),
        (("c", 1, 2, 6), ("c", 6, 7, 1)),
        (("c", 2, 3, 5), ("c", 5, 6, 2)),
        (("c", 3, 4, 4), ("c", 4, 5, 3)),
    ),
) * 2
SECOND = (
    ((("c", 15, 0, 4),), (("c", 15, 4, 4),), (("r", 8, 7, 4),), (("r", 12, 7, 3),)),
    tuple((("c", 15, 2 * k, 2),) for k in range(ROUTES)),
)
HOLD = 11


def zero_window(win, first_col, row):
    def corner(q, carry):
        win[16 + q, pl.ds(0, 8)] = jnp.zeros((8, T, T), BF)
        win[q, pl.ds(16, 8)] = jnp.zeros((8, T, T), BF)
        return carry

    lax.fori_loop(0, 8, corner, 0)
    for u in range(8):
        win[8 + u, pl.ds(0, u + 1)] = jnp.zeros((u + 1, T, T), BF)
        if u < 7:
            win[8 + u, pl.ds(17 + u, 7 - u)] = jnp.zeros((7 - u, T, T), BF)
    win[23, pl.ds(16, 8)] = jnp.zeros((8, T, T), BF)
    for q in range(8):
        win[first_col + q, row] = jnp.zeros((T, T), BF)


def zero_side(win, first_col, row):
    def one(q, carry):
        win[first_col + q, pl.ds(row, 8)] = jnp.zeros((8, T, T), BF)
        return carry

    lax.fori_loop(0, 16, one, 0)


def pack(table, line, lane, raw, dst, base, first, end):
    def one(col, carry):
        for t in range(R):
            slot = table[line + col, lane + t]
            tile = raw[jnp.maximum(slot, 0), t]
            dst[col, base + t] = jnp.where(slot >= 0, tile, jnp.zeros_like(tile))
        return carry

    lax.fori_loop(first, end, one, 0)


def band_step(left, win, pair, rows, start, depth, put):
    lhs = jnp.concatenate(
        [left[start + q, pl.ds(2 * rows, 2)].reshape(2 * T, T) for q in range(depth)], axis=1
    )
    rhs = jnp.concatenate(
        [win[2 * pair + h, pl.ds(start, depth)].reshape(depth * T, T) for h in range(2)], axis=1
    )
    total = jnp.dot(lhs, rhs, preferred_element_type=jnp.float32)
    for h in range(2):
        for m in range(2):
            put(2 * pair + h, 2 * rows + m, total[m * T : (m + 1) * T, h * T : (h + 1) * T])


def fused_kernel(
    last, width, side, new_index, zpat, fpat, ppat, rpat, z, f, incoming,
    win, pwin, left, turned, orth, sem_z, sem_f, sem_o,
    zus, zur, zds, zdr, pus, pur, pds, pdr, hold, es, er, hs, hr, xs, xr, ready,
    pats, lines, table, sem_p, sem_t,
):
    mesh_row = lax.axis_index("row")
    mesh_col = lax.axis_index("col")
    device = mesh_row * width + mesh_col
    has_low = device > 0
    has_high = device < last
    wide = (device < 2) | (device > last - 2)
    is_first = device == 0
    is_last = device == last

    lane = mesh_col * R
    group = pl.multiple_of(mesh_row * width * R, width * R)
    pat_loads = [
        pltpu.make_async_copy(pat.at[:, pl.ds(group, width * R)], pats.at[k], sem_p.at[k])
        for k, pat in enumerate((zpat, fpat, ppat, rpat))
    ]
    for copy in pat_loads:
        copy.start()
    loads = [
        pltpu.make_async_copy(z.at[t], orth.at[pl.ds(0, K), t], sem_z.at[t]) for t in range(R)
    ]
    floads = [
        pltpu.make_async_copy(f.at[t], turned.at[pl.ds(0, K), t], sem_f.at[t]) for t in range(R)
    ]
    for copy in loads:
        copy.start()

    def place(dev):
        return (dev // width, lax.rem(dev, width))

    def peer(o):
        col = lax.rem(mesh_col // side + o[0], side) * side + lax.rem(mesh_col + o[1], side)
        return col

    def relays(receiver):
        row, col = divmod(receiver, width)
        rows = (last + 1) // width
        return [
            row * width + (col + side) % width,
            row * width + (col - side) % width,
            (row + 2) % rows * width + col,
            (row - 2) % rows * width + col,
        ]

    flows = [(0, 1, True, FIRST), (last, last - 1, False, LAST), (1, 0, False, SECOND)]

    def pieces(flow, stage):
        return [
            (route, 3 * route + q, piece, sum(p[3] for p in group[:q]))
            for route, group in enumerate(flow[3][stage])
            for q, piece in enumerate(group)
        ]

    def part(buf, piece, shift, base):
        kind, col, row, count = piece
        if kind == "c":
            return buf.at[col + shift, pl.ds(base + row, count)]
        return buf.at[pl.ds(col + shift, count), base + row]

    def to_relay(buf, flow, stage, route, index, piece, off):
        return pltpu.make_async_remote_copy(
            src_ref=part(buf, piece, 0, 8),
            dst_ref=hold.at[stage, pl.ds(off, piece[3])],
            send_sem=es.at[stage, index],
            recv_sem=hr.at[stage, index % 3],
            device_id=divmod(relays(flow[1])[route], width),
            device_id_type=MESH,
        )

    def to_end(buf, flow, stage, index, piece, off):
        shift, base = (-8, 0) if flow[2] else (8, 16)
        return pltpu.make_async_remote_copy(
            src_ref=hold.at[stage, pl.ds(off, piece[3])],
            dst_ref=part(buf, piece, shift, base),
            send_sem=hs.at[stage, index % 3],
            recv_sem=er.at[stage, index],
            device_id=divmod(flow[1], width),
            device_id_type=MESH,
        )

    def edge_start(buf, stage, which, kinds):
        flow = flows[which]

        @pl.when(device == flow[0])
        def _():
            for route, index, piece, off in pieces(flow, stage):
                if piece[0] in kinds:
                    to_relay(buf, flow, stage, route, index, piece, off).start()

    def edge_forward(buf, stage):
        for flow in flows:
            for k, relay in enumerate(relays(flow[1])):

                @pl.when(device == relay)
                def _():
                    mine = [p for p in pieces(flow, stage) if p[0] == k]
                    for route, index, piece, off in mine:
                        to_relay(buf, flow, stage, route, index, piece, off).wait_recv()
                        to_end(buf, flow, stage, index, piece, off).start()

    def edge_receive(buf, stage, which):
        flow = flows[which]

        @pl.when(device == flow[1])
        def _():
            for route, index, piece, off in pieces(flow, stage):
                to_end(buf, flow, stage, index, piece, off).wait_recv()

    def edge_drain(buf, stage):
        for flow in flows:

            @pl.when(device == flow[0])
            def _():
                for route, index, piece, off in pieces(flow, stage):
                    to_relay(buf, flow, stage, route, index, piece, off).wait_send()

            for k, relay in enumerate(relays(flow[1])):

                @pl.when(device == relay)
                def _():
                    for route, index, piece, off in pieces(flow, stage):
                        if route == k:
                            to_end(buf, flow, stage, index, piece, off).wait_send()

    barrier = pltpu.get_barrier_semaphore()
    extra = jnp.int32(0)
    for flow in flows:
        extra = extra + jnp.where(device == flow[0], 2, 0)
        for relay in relays(flow[1])[2:]:
            extra = extra + jnp.where(device == relay, 1, 0)

            @pl.when(device == relay)
            def _():
                pl.semaphore_signal(
                    barrier, inc=1, device_id=divmod(flow[0], width), device_id_type=MESH
                )

            @pl.when(device == flow[1])
            def _():
                pl.semaphore_signal(
                    barrier, inc=1, device_id=divmod(relay, width), device_id_type=MESH
                )

    for o in OFFSETS:
        pl.semaphore_signal(barrier, inc=1, device_id=(mesh_row, peer(o)), device_id_type=MESH)

    zero_window(win, 16, 23)

    for copy in pat_loads:
        copy.wait()
    slot_ids = lax.broadcasted_iota(jnp.int32, (K, width * R), 0)
    for k in range(3):
        for col in range(C):
            hit = pats[k] == device * R + (col - 8)
            lines[k * C + col] = jnp.max(jnp.where(hit, slot_ids, -1), axis=0)
    lines[pl.ds(3 * C + 8, 8)] = jnp.zeros((8, width * R), jnp.int32)
    there = jnp.clip(pats[3] - (device * R - 8), 0, C)
    lines[pl.ds(3 * C, K)] = jnp.where(pats[3] >= 0, there, C)
    to_scalars = pltpu.make_async_copy(lines, table, sem_t)
    to_scalars.start()

    @pl.when(is_first)
    def _():
        zero_side(win, 0, 0)

    @pl.when(is_last)
    def _():
        zero_side(win, 8, 16)

    @pl.when(has_low)
    def _():
        pl.semaphore_signal(barrier, inc=1, device_id=place(device - 1), device_id_type=MESH)

    @pl.when(has_high)
    def _():
        pl.semaphore_signal(barrier, inc=1, device_id=place(device + 1), device_id_type=MESH)

    def send(buf, col, row, rows, to_col, to_row, ssem, rsem, dev):
        return pltpu.make_async_remote_copy(
            src_ref=buf.at[col, pl.ds(8 + row, rows)],
            dst_ref=buf.at[to_col, pl.ds(to_row, rows)],
            send_sem=ssem,
            recv_sem=rsem,
            device_id=place(dev),
            device_id_type=MESH,
        )

    def up_col(buf, col, ss, rs, skip):
        return send(
            buf, col, skip, 8 - skip, col - 8, skip, ss.at[col - 8], rs.at[col - 8], device + 1
        )

    def down_col(buf, col, ss, rs, skip):
        return send(buf, col, 0, 8 - skip, col + 8, 16, ss.at[col], rs.at[col], device - 1)

    def up_tri(buf, ss, rs):
        return [
            send(buf, 16 + u, u + 1, 7 - u, 8 + u, u + 1, ss.at[8 + u], rs.at[8 + u], device + 1)
            for u in range(7)
        ]

    def down_tri(buf, ss, rs):
        return [
            send(buf, u, 0, u + 1, 8 + u, 16, ss.at[u], rs.at[u], device - 1)
            for u in range(7, -1, -1)
        ]

    def start_all(copies):
        for copy in copies:
            copy.start()

    to_scalars.wait()
    for copy in loads:
        copy.wait()
    for copy in floads:
        copy.start()
    pack(table, 0, lane, orth, win, 8, 8, 16)

    neighbours = has_low.astype(jnp.int32) + has_high.astype(jnp.int32)
    pl.semaphore_wait(barrier, width - 1 + neighbours + extra)

    @pl.when(has_high)
    def _():
        start_all([up_col(win, col, zus, zur, 0) for col in range(8, 16)])

    @pl.when(has_low)
    def _():
        start_all([down_col(win, col, zds, zdr, 1) for col in range(14, 7, -1)])

    pack(table, 0, lane, orth, win, 8, 0, 8)
    pack(table, 0, lane, orth, win, 8, 16, C)
    for which in range(3):
        edge_start(win, 0, which, "cr")

    zero_window(pwin, 0, 0)

    def clear(q, carry):
        pwin[q, pl.ds(8, 8)] = jnp.zeros((8, T, T), BF)
        pwin[16 + q, pl.ds(8, 8)] = jnp.zeros((8, T, T), BF)
        return carry

    lax.fori_loop(0, 8, clear, 0)
    orth[C] = jnp.zeros((R, T, T), BF)

    @pl.when(is_first)
    def _():
        zero_side(pwin, 0, 0)

    @pl.when(is_last)
    def _():
        zero_side(pwin, 8, 16)

    @pl.when(has_high)
    def _():
        start_all(up_tri(win, zus, zur))

    @pl.when(has_low)
    def _():
        start_all(down_tri(win, zds, zdr))

    for copy in floads:
        copy.wait()
    pack(table, C, lane, turned, left, 0, 0, C)

    def outer(lhs, buf, us, ur, ds, dr, put, second):
        skip_up, skip_down = (1, 0) if second else (0, 1)

        def one(q, carry):
            half = q // 2
            if second:
                pair = jnp.where(lax.rem(q, 2) == 0, 3 - half, 8 + half)
            else:
                pair = jnp.where(lax.rem(q, 2) == 0, half, 11 - half)

            @pl.when((pair < 4) & has_low)
            def _():
                up_col(buf, 2 * pair + 8, us, ur, skip_up).wait_recv()
                up_col(buf, 2 * pair + 9, us, ur, skip_up).wait_recv()

            @pl.when((pair >= 8) & has_high)
            def _():
                down_col(buf, 2 * pair - 8, ds, dr, skip_down).wait_recv()

            @pl.when((pair >= 8) & (pair < 11) & has_high)
            def _():
                down_col(buf, 2 * pair - 7, ds, dr, skip_down).wait_recv()

            @pl.when(pair == 11)
            def _():
                edge_receive(buf, int(second), 2)

            if not second:

                @pl.when(q == 2)
                def _():
                    edge_forward(buf, 0)

            low = jnp.where(pair < 4, 0, pair - 8)
            low = jnp.where(is_first, jnp.where(pair < 4, 4, 0), low)
            low = jnp.where(is_last, jnp.where(pair < 4, 0, 4), low)
            high = jnp.where(is_first | is_last, 4, jnp.minimum(pair, 3) + 1)
            start = jnp.where(pair < 4, 0, 6)

            def rows_step(rows, inner):
                band_step(lhs, buf, pair, rows, start, 18, put)
                return inner

            return lax.fori_loop(low, high, rows_step, carry)

        lax.fori_loop(0, 8, one, 0)

    def wait_middle(buf, us, ur, ds, dr, stage):
        @pl.when(has_low)
        def _():
            for copy in up_tri(buf, us, ur):
                copy.wait_recv()

        @pl.when(has_high)
        def _():
            for copy in down_tri(buf, ds, dr):
                copy.wait_recv()

        edge_receive(buf, stage, 0)
        edge_receive(buf, stage, 1)

    def middle(lhs, buf, put, after):
        def one(q, carry):
            pair = jnp.where(lax.rem(q, 2) == 0, 7 - q // 2, 4 + q // 2)

            @pl.when(jnp.logical_not(wide))
            def _():
                def rows_step(rows, inner):
                    band_step(lhs, buf, pair, rows, 2 * pair - 8, 18, put)
                    return inner

                lax.fori_loop(0, 4, rows_step, 0)

            @pl.when(wide)
            def _():
                def rows_step(rows, inner):
                    band_step(lhs, buf, pair, rows, 0, C, put)
                    return inner

                lax.fori_loop(0, 4, rows_step, 0)

            after(q)
            return carry

        lax.fori_loop(0, 4, one, 0)

    def put_product(col, row, value):
        pwin[col, 8 + row] = jnp.where(table[2 * C + col, lane + row] >= 0, value, 0.0).astype(BF)

    outer(left, win, zus, zur, zds, zdr, put_product, False)

    @pl.when(has_high)
    def _():
        start_all(up_tri(pwin, pus, pur))

    @pl.when(has_low)
    def _():
        start_all(down_tri(pwin, pds, pdr))

    wait_middle(win, zus, zur, zds, zdr, 0)

    edge_start(pwin, 1, 0, "c")
    edge_start(pwin, 1, 1, "c")

    def send_up(pair):
        @pl.when(has_high)
        def _():
            start_all([up_col(pwin, 2 * pair + h, pus, pur, 1) for h in range(2)])

    def send_down(pair):
        @pl.when(has_low)
        def _():
            down_col(pwin, 2 * pair, pds, pdr, 0).start()

        @pl.when(has_low & (pair < 7))
        def _():
            down_col(pwin, 2 * pair + 1, pds, pdr, 0).start()

    def send_ready(q):
        @pl.when(q == 1)
        def _():
            send_up(7)
            edge_start(pwin, 1, 2, "c")

        @pl.when(q == 2)
        def _():
            send_down(4)

        @pl.when(q == 3)
        def _():
            send_up(6)

    middle(left, win, put_product, send_ready)

    def turn(k, carry):
        for a in range(R):
            turned[k, a] = win[8 + a, k].T
        return carry

    lax.fori_loop(0, 2, turn, 0)
    send_up(5)
    send_down(5)
    send_up(4)
    send_down(6)
    send_down(7)

    edge_start(pwin, 1, 0, "r")
    lax.fori_loop(2, C, turn, 0)
    edge_forward(pwin, 1)

    def put_orth(col, row, value):
        orth[col, row] = value.astype(BF)

    wait_middle(pwin, pus, pur, pds, pdr, 1)
    middle(turned, pwin, put_orth, lambda q: None)
    outer(turned, pwin, pus, pur, pds, pdr, put_orth, True)

    def wait_sends(buf, us, ur, ds, dr, product):
        def drain(copies):
            for copy in copies:
                copy.wait_send()

        @pl.when(has_high)
        def _():
            drain([up_col(buf, col, us, ur, product) for col in range(8, 16)])
            drain(up_tri(buf, us, ur))

        @pl.when(has_low)
        def _():
            drain([down_col(buf, col, ds, dr, 1 - product) for col in range(8, 15)])
            drain(down_tri(buf, ds, dr))

        edge_drain(buf, product)

    def stage(e):
        row = jnp.int32(0)
        for t in range(R):
            there = lax.rem(new_index[device * R + t] // R, width)
            row = jnp.where(there == e, t, row)
        for s in range(K):
            win[e, s] = orth[table[3 * C + s, lane + row], row]

    wait_sends(win, zus, zur, zds, zdr, 0)

    def packet(q, p):
        there = peer(OFFSETS[q])
        slots = pl.ds(p * K // PARTS, K // PARTS)
        return pltpu.make_async_remote_copy(
            src_ref=win.at[there, slots],
            dst_ref=incoming.at[mesh_col, slots],
            send_sem=xs.at[p, q],
            recv_sem=xr.at[p, q],
            device_id=(mesh_row, there),
            device_id_type=MESH,
        )

    count = width - 1
    for o in OFFSETS:
        pl.semaphore_signal(ready, inc=1, device_id=(mesh_row, peer(o)), device_id_type=MESH)
    for q in range(count):
        stage(peer(OFFSETS[q]))
    stage(mesh_col)
    pl.semaphore_wait(ready, count)
    for p in range(PARTS):
        for q in range(count):
            packet(q, p).start()
    mine = pltpu.make_async_copy(win.at[mesh_col, pl.ds(0, K)], incoming.at[mesh_col], sem_o)
    mine.start()
    wait_sends(pwin, pus, pur, pds, pdr, 1)
    mine.wait()
    for p in range(PARTS):
        for q in range(count):
            packet(q, p).wait()


def take_kernel(width, new_index, incoming, out, held, sem_in, sem_out):
    device = lax.axis_index("row") * width + lax.axis_index("col")
    group = device // width * width

    def row(q, carry):
        def look(j, found):
            hit = new_index[(group + j) * R + q] == device * R + q
            return jnp.where(hit, j, found)

        source = lax.fori_loop(0, width, look, 0)
        pltpu.make_async_copy(incoming.at[source], held.at[q], sem_in.at[q]).start()
        return carry

    lax.fori_loop(0, R, row, 0)
    outs = []
    for q in range(R):
        pltpu.make_async_copy(incoming.at[0], held.at[q], sem_in.at[q]).wait()
        outs.append(pltpu.make_async_copy(held.at[q], out.at[q], sem_out.at[q]))
        outs[q].start()
    for copy in outs:
        copy.wait()


def body(
    fock_tiles, fock_pattern, basis_tiles, basis_pattern, product_pattern, result_pattern, new_index
):
    width = lax.axis_size("col")
    last = lax.axis_size("row") * width - 1
    dma = pltpu.SemaphoreType.DMA
    incoming = pl.pallas_call(
        functools.partial(fused_kernel, last, width, 4),
        out_shape=jax.ShapeDtypeStruct((width, K, T, T), BF),
        in_specs=[SMEM] + [ANY] * 6,
        out_specs=ANY,
        scratch_shapes=[
            pltpu.VMEM((C, C, T, T), BF),
            pltpu.VMEM((C, C, T, T), BF),
            pltpu.VMEM((C, R, T, T), BF),
            pltpu.VMEM((C, R, T, T), BF),
            pltpu.VMEM((C + 1, R, T, T), BF),
            dma((R,)),
            dma((R,)),
            dma,
        ]
        + [dma((15,))] * 8
        + [pltpu.VMEM((2, HOLD, T, T), BF)]
        + [dma((2, 3 * ROUTES))] * 2
        + [dma((2, 3))] * 2
        + [dma((PARTS, width - 1))] * 2
        + [pltpu.SemaphoreType.REGULAR]
        + [pltpu.VMEM((4, K, width * R), jnp.int32)]
        + [pltpu.VMEM((3 * C + 16, width * R), jnp.int32)]
        + [pltpu.SMEM((3 * C + 16, width * R), jnp.int32)]
        + [dma((4,)), dma],
        compiler_params=pltpu.CompilerParams(
            vmem_limit_bytes=VMEM_LIMIT, collective_id=0, has_side_effects=True
        ),
        name="fused",
    )(
        new_index,
        basis_pattern.T,
        fock_pattern.T,
        product_pattern.T,
        result_pattern.T,
        basis_tiles,
        fock_tiles,
    )
    return pl.pallas_call(
        functools.partial(take_kernel, width),
        out_shape=jax.ShapeDtypeStruct((R, K, T, T), BF),
        in_specs=[SMEM, ANY],
        out_specs=ANY,
        scratch_shapes=[pltpu.VMEM((R, K, T, T), BF), dma((R,)), dma((R,))],
        name="take",
    )(new_index, incoming)


def solution(mesh):
    placed = (
        P(("row", "col"), None, None, None),
        P(),
        P(("row", "col"), None, None, None),
        P(),
        P(),
        P(),
        P(),
    )
    return jax.shard_map(
        body,
        mesh=mesh,
        in_specs=placed,
        out_specs=P(("row", "col"), None, None, None),
        check_vma=False,
    )
```
